512 devices in a mesh: tm: 16 (over z, core), space: 32 (over y, x).
Axes of the slice: x: 4, y: 8, z: 8, core: 2. Of those that a mesh axis runs over, the one named last changes fastest.
Arguments:
- tokens: bfloat16 [131072, 1024], P(('tm', 'space')), may hold values from -6 to 6
- latents: bfloat16 [512, 1024], replicated, may hold values from -300 to 300
- up_weight: bfloat16 [1024, 4096], P(None, 'tm'), may hold values from -0.1875 to 0.1875
- down_weight: bfloat16 [4096, 1024], P('tm'), may hold values from -0.09375 to 0.09375
Outputs:
- new_tokens: bfloat16 [131072, 1024], P(('tm', 'space'))
- new_latents: bfloat16 [512, 1024], P('space')
The draws below stay inside these ranges and needn't reach their ends.
All inputs are finite; a program needn't handle non-finite values.
Results may differ from the reference program's by a relative error of at most 0.012.
The reference program's roundings to bfloat16 on the way count: a program that leaves them out, or rounds other values in their place, can miss the bound.
Values may be sent and summed in bfloat16 or wider, within the bound.
No kernel may reach another device: no remote copies, remote signals or barrier semaphores. Data moves between devices by JAX's collectives and lax.ppermute only.
A program may use at most 64 MiB of HBM per device.

```python
import jax
import jax.numpy as jnp
from jax import lax

D = 1024
H = 16
FF = 4096
NL = 512
TOK_DEV = 256
TOKENS = 131072


def draw_latents(key, part):
    base = jnp.clip(jax.random.normal(jax.random.fold_in(key, 11), (NL, D), jnp.float32), -5.0, 5.0)
    values = base * 6.0
    return values.astype(jnp.bfloat16)


def block_levels(key, extent, pieces, smallest, top_value):
    def one(dim, shards_of):
        draws = jax.random.uniform(jax.random.fold_in(jax.random.fold_in(key, 6), dim), (shards_of,), jnp.float32, smallest / len(pieces), top_value / len(pieces))
        return jnp.repeat(jnp.exp(draws), extent[dim] // shards_of).reshape((-1,) + (1,) * (len(extent) - dim - 1))

    loudness = one(*pieces[0])
    for cut in pieces[1:]:
        loudness = loudness * one(*cut)
    return loudness


def scatter_about(key, extent, width, bound, shards=(), kind=jnp.bfloat16):
    gain = block_levels(key, extent, shards, -0.22, 0.18) if shards else 1.0
    array = jax.random.normal(key, extent, jnp.float32) * width * gain
    return jnp.minimum(jnp.maximum(array, -bound), bound).astype(kind)


def setup_inputs(seed: int = 0) -> dict:
    key_of = jax.random.split(jax.random.key(seed), 5)
    return {
        "tokens": scatter_about(key_of[0], (TOKENS, D), 1.0, 6.0, ((0, 512),)),
        "latents": draw_latents(jax.random.fold_in(key_of[4], 71), 0),
        "up_weight": scatter_about(key_of[2], (D, FF), D ** -0.5, 0.1875, ((1, 16),)),
        "down_weight": scatter_about(key_of[3], (FF, D), FF ** -0.5, 0.09375, ((0, 16),)),
    }


epsilon = 1e-05
head_groups = 4

def layer_norm(values):
    center = values - lax.optimization_barrier(jnp.mean(values, axis=-1, keepdims=True))
    spread = lax.optimization_barrier(jnp.mean(center * center, axis=-1, keepdims=True))
    return center * lax.rsqrt(spread + epsilon)

def wire_round(values):
    rounded = lax.optimization_barrier(values.astype(jnp.bfloat16))
    return rounded.astype(jnp.float32)

def split_heads(matrix, head_count):
    row_count = matrix.shape[0]
    head_size = matrix.shape[1] // head_count
    return matrix.reshape(row_count, head_groups, head_count // head_groups, head_size).transpose(1, 2, 0, 3)

def per_head(weighted, factor):
    row_count = weighted.shape[0]
    return (weighted.reshape(row_count, factor.shape[1], -1) * factor[:, :, None]).reshape(row_count, weighted.shape[1])

def read_peaks(queries, keys_tok, head_count):
    score_scale = (queries.shape[1] // head_count) ** (-0.5)

    def one_group(operands):
        query_part, key_part = operands
        scores = jnp.einsum('hld,htd->hlt', query_part.astype(jnp.float32), key_part.astype(jnp.float32)) * score_scale
        return lax.optimization_barrier(jnp.max(scores, axis=-1))
    row_peak = lax.map(one_group, (split_heads(queries, head_count), split_heads(keys_tok, head_count)))
    return row_peak.reshape(head_count, queries.shape[0]).T

def read_partial(queries, keys_tok, tokens, head_count):
    score_scale = (queries.shape[1] // head_count) ** (-0.5)

    def one_group(operands):
        query_part, key_part, value_part = operands
        scores = jnp.einsum('hld,htd->hlt', query_part.astype(jnp.float32), key_part.astype(jnp.float32)) * score_scale
        row_peak = lax.optimization_barrier(jnp.max(scores, axis=-1))
        weights = jnp.exp(scores - row_peak[..., None])
        row_total = lax.optimization_barrier(jnp.sum(weights, axis=-1))
        rounded = wire_round(weights)
        weighted = jnp.einsum('hlt,htd->lhd', rounded, value_part.astype(jnp.float32))
        return (row_peak, row_total, weighted)
    row_peak, row_total, weighted = lax.map(one_group, (split_heads(queries, head_count), split_heads(keys_tok, head_count), split_heads(tokens, head_count)))
    latent_count = queries.shape[0]
    row_peak = row_peak.reshape(head_count, latent_count).T
    row_total = row_total.reshape(head_count, latent_count).T
    weighted = weighted.transpose(1, 0, 2, 3).reshape(latent_count, queries.shape[1])
    return (row_peak, row_total, weighted)

def write_tokens(keys_tok, all_latents, tokens, head_count):
    score_scale = (all_latents.shape[1] // head_count) ** (-0.5)
    write_values = layer_norm(all_latents.astype(jnp.float32)).astype(jnp.bfloat16)

    def one_group(operands):
        query_part, key_part, value_part = operands
        scores = jnp.einsum('htd,hld->htl', query_part.astype(jnp.float32), key_part.astype(jnp.float32)) * score_scale
        weights = jnp.exp(scores - lax.optimization_barrier(jnp.max(scores, axis=-1, keepdims=True)))
        shares = (weights / lax.optimization_barrier(jnp.sum(weights, axis=-1, keepdims=True))).astype(jnp.bfloat16)
        return jnp.einsum('htl,hld->thd', shares.astype(jnp.float32), value_part.astype(jnp.float32))
    attended = lax.map(one_group, (split_heads(keys_tok, head_count), split_heads(all_latents, head_count), split_heads(write_values, head_count)))
    token_count = tokens.shape[0]
    attended = attended.transpose(1, 0, 2, 3).reshape(token_count, tokens.shape[1])
    return (tokens.astype(jnp.float32) + attended).astype(jnp.bfloat16)

def reference(tokens, latents, up_weight, down_weight):
    keys_tok = layer_norm(tokens.astype(jnp.float32)).astype(jnp.bfloat16)
    block_count = TOKENS // TOK_DEV
    key_blocks = keys_tok.reshape(block_count, TOK_DEV, D)
    token_blocks = tokens.reshape(block_count, TOK_DEV, D)

    def block_peak_of(key_block):
        return read_peaks(latents, key_block, H)
    block_peaks = lax.map(block_peak_of, key_blocks)
    read_peak = lax.optimization_barrier(jnp.max(block_peaks, axis=0))

    def absorb(carry, operands):
        total_sum, weighted_sum = carry
        block_peak, row_total, weighted = read_partial(latents, operands[0], operands[1], H)
        factor = jnp.exp(block_peak - read_peak)
        total_sum = total_sum + wire_round(row_total * factor)
        weighted_sum = weighted_sum + wire_round(per_head(weighted, factor))
        return ((total_sum, weighted_sum), None)
    initial = (jnp.zeros((NL, H), jnp.float32), jnp.zeros((NL, D), jnp.float32))
    (row_total, weighted), _ = lax.scan(absorb, initial, (key_blocks, token_blocks))
    read_out = (weighted.reshape(NL, H, -1) / row_total[:, :, None]).reshape(NL, D)
    middle = latents.astype(jnp.float32) + read_out
    normed = layer_norm(middle).astype(jnp.bfloat16)
    hidden = jax.nn.gelu(jnp.dot(normed, up_weight, preferred_element_type=jnp.float32), approximate=False).astype(jnp.bfloat16)
    new_latents = (middle + jnp.dot(hidden, down_weight, preferred_element_type=jnp.float32)).astype(jnp.bfloat16)

    def write_block(operands):
        return write_tokens(operands[0], new_latents, operands[1], H)
    new_tokens = lax.map(write_block, (key_blocks, token_blocks)).reshape(TOKENS, D)
    return (new_tokens, new_latents)
```

```python
import functools
import math

import jax
import jax.numpy as jnp
from jax import lax
from jax.experimental import pallas as pl
from jax.experimental.pallas import tpu as pltpu
from jax.sharding import Mesh
from jax.sharding import PartitionSpec as P

H = 16
HD = 64
Z, CORE = "tm_0", "tm_1"
SPACE = ("space_0", "space_1")
TM = (Z, CORE)
TM_SPACE = TM + SPACE
epsilon = 1e-05
LOG2E = math.log2(math.e)
STATS = 128
f32, bf16 = jnp.float32, jnp.bfloat16
HIGHEST = lax.Precision.HIGHEST


def layer_norm(values):
    center = values - jnp.mean(values, axis=-1, keepdims=True)
    spread = jnp.mean(center * center, axis=-1, keepdims=True)
    return center * lax.rsqrt(spread + epsilon)


def cols_dot(a, b):
    return lax.dot_general(a, b, (((1,), (1,)), ((), ())), preferred_element_type=f32)


def attend(keys, queries, values_t, head, state):
    pair = pl.ds((head // 2) * 2 * HD, 2 * HD)
    query = queries[:, pair]
    lane = lax.broadcasted_iota(jnp.int32, query.shape, 1)
    query = jnp.where((lane >= HD) == (head % 2 == 1), query, jnp.zeros_like(query))
    scores = cols_dot(keys[:, pair], query) * (HD**-0.5 * LOG2E)
    peak = jnp.max(scores, axis=0, keepdims=True)
    if state is not None:
        peak = jnp.maximum(peak, state[0])
    weights = jnp.exp2(scores - peak)
    total = jnp.sum(weights, axis=0, keepdims=True)
    summed = jnp.dot(
        values_t[head * HD : (head + 1) * HD, :], weights.astype(bf16), preferred_element_type=f32
    )
    if state is not None:
        old = jnp.exp2(state[0] - peak)
        total = total + state[1] * old
        summed = summed + state[2] * old
    return peak, total, summed


def load_state(state, head):
    peaks, totals, sums = state
    return peaks[head : head + 1, :], totals[head : head + 1, :], sums[head * HD : (head + 1) * HD, :]


def read_first(tokens, latents, keys, peaks, totals, sums, values_t):
    value = tokens[...]
    keys[...] = layer_norm(value.astype(f32)).astype(bf16)
    values_t[...] = value.T
    for head in range(H):
        peak, total, summed = attend(keys, latents, values_t, head, None)
        peaks[head : head + 1, :] = peak
        totals[head : head + 1, :] = total
        sums[head * HD : (head + 1) * HD, :] = summed


def read_second(tokens, latents, peaks, totals, sums, packed, keys, values_t, packed_t):
    value = tokens[...]
    keys[...] = layer_norm(value.astype(f32)).astype(bf16)
    values_t[...] = value.T
    width = H * HD
    packed_t[width:, :] = jnp.zeros_like(packed_t[width:, :])
    for head in range(H):
        state = load_state((peaks, totals, sums), head)
        peak, total, summed = attend(keys, latents, values_t, head, state)
        sent = peak.astype(bf16).astype(f32)
        scale = jnp.exp2(peak - sent)
        packed_t[head * HD : (head + 1) * HD, :] = summed * scale
        packed_t[width + head : width + head + 1, :] = total * scale
        packed_t[width + H + head : width + H + head + 1, :] = sent
    packed[...] = packed_t[...].T.reshape(packed.shape).astype(bf16)


def expand(factor):
    head = lax.broadcasted_iota(jnp.int32, (H, H * HD), 0)
    lane = lax.broadcasted_iota(jnp.int32, (H, H * HD), 1)
    spread = (lane // HD == head).astype(f32)
    return jnp.dot(factor, spread, precision=HIGHEST, preferred_element_type=f32)


def combine(tiles):
    n, rows, _ = tiles.shape
    width = H * HD
    totals, peaks = tiles[:, :, width : width + H], tiles[:, :, width + H : width + 2 * H]
    peak = jnp.max(peaks, axis=0)
    factor = jnp.exp2(peaks - peak[None])
    total = jnp.sum(totals * factor, axis=0)
    wide = expand(factor.reshape(n * rows, H)).reshape(n, rows, width)
    return jnp.sum(tiles[:, :, :width] * wide, axis=0), total, peak


def combine_space(arrived, out):
    summed, total, peak = combine(arrived[...].astype(f32))
    rest = jnp.zeros((summed.shape[0], STATS - 2 * H), f32)
    tile = jnp.concatenate([summed, total, peak, rest], axis=1).astype(bf16)
    out[...] = jnp.broadcast_to(tile[None], out.shape)


def mlp(position, arrived, latents, up, down, out, middle_own):
    tiles = arrived[...].astype(f32)
    rows = tiles.shape[1]
    tiles = tiles.reshape(tiles.shape[0] // 2, 2 * rows, tiles.shape[2])
    summed, total, _ = combine(tiles)
    read_out = summed * expand(1.0 / total)
    middle = latents[...].astype(f32).reshape(2 * rows, H * HD) + read_out
    normed = layer_norm(middle).astype(bf16)
    hidden = jnp.dot(normed, up[...], preferred_element_type=f32)
    hidden = (0.5 * hidden * (1.0 + lax.erf(hidden * math.sqrt(0.5)))).astype(bf16)
    part = jnp.dot(hidden, down[...], preferred_element_type=f32)
    part = part.reshape(1, 2, rows, H * HD).astype(bf16)
    out[...] = jnp.broadcast_to(part, out.shape)
    middle_own[...] = jnp.where(position[1] == 0, middle[:rows], middle[rows:])


def finish(parts, middle, out):
    new = (middle[...] + jnp.sum(parts[...].astype(f32), axis=0)).astype(bf16)
    out[...] = jnp.broadcast_to(new[None], out.shape)


def prepare_write(latents, lat, values_t):
    new = latents[...].astype(f32)
    new = new.reshape(new.shape[0] * new.shape[1], new.shape[2])
    lat[...] = new.astype(bf16)
    values_t[...] = layer_norm(new).T.astype(bf16)


def write_first(latents, keys, peaks, totals, sums, lat, values_t):
    prepare_write(latents, lat, values_t)
    for head in range(H):
        peak, total, summed = attend(lat, keys, values_t, head, None)
        peaks[head : head + 1, :] = peak
        totals[head : head + 1, :] = total
        sums[head * HD : (head + 1) * HD, :] = summed


def write_second(latents, keys, tokens, peaks, totals, sums, out, lat, values_t, out_t):
    prepare_write(latents, lat, values_t)
    for head in range(H):
        state = load_state((peaks, totals, sums), head)
        _, total, summed = attend(lat, keys, values_t, head, state)
        out_t[head * HD : (head + 1) * HD, :] = summed * (1.0 / total)
    out[...] = (tokens[...].astype(f32) + out_t[...].T).astype(bf16)


def call(kernel, outs, scratch=(), in_specs=None, prefetch=0, flops=0, **kw):
    whole = pl.BlockSpec(memory_space=pltpu.VMEM)
    single = not isinstance(outs, (list, tuple))
    out_list = [outs] if single else list(outs)
    spec = dict(
        out_shape=outs,
        compiler_params=pltpu.CompilerParams(vmem_limit_bytes=48 << 20),
        name=kernel.__name__,
        cost_estimate=pl.CostEstimate(flops=flops, transcendentals=flops // 256, bytes_accessed=1 << 20),
    )
    if prefetch:
        grid_spec = pltpu.PrefetchScalarGridSpec(
            num_scalar_prefetch=prefetch,
            grid=(1,),
            in_specs=in_specs,
            out_specs=whole if single else [whole] * len(out_list),
            scratch_shapes=list(scratch),
        )
        return pl.pallas_call(kernel, grid_spec=grid_spec, **spec)
    return pl.pallas_call(
        kernel,
        in_specs=[whole] * in_specs,
        out_specs=whole if single else [whole] * len(out_list),
        scratch_shapes=list(scratch),
        **spec,
    )


def on_device(tokens, latents, up_weight, down_weight):
    shape = jax.ShapeDtypeStruct
    n_space, n_z = lax.axis_size(SPACE), lax.axis_size(Z)
    count, width = tokens.shape
    half = latents.shape[0] // 2
    rows = half // n_space
    core, place = lax.axis_index(CORE), lax.axis_index(SPACE)
    heavy = 4 * half * count * width

    other = lax.ppermute(tokens, CORE, [(0, 1), (1, 0)])
    own = lax.dynamic_slice_in_dim(latents, core * half, half, 0)
    state = [shape((H, half), f32), shape((H, half), f32), shape((width, half), f32)]
    keys, *part = call(
        read_first,
        [shape((count, width), bf16), *state],
        [pltpu.VMEM((width, count), bf16)],
        in_specs=2,
        flops=heavy,
    )(tokens, own)
    packed = call(
        read_second,
        shape((n_space, rows, width + STATS), bf16),
        [
            pltpu.VMEM((count, width), bf16),
            pltpu.VMEM((width, count), bf16),
            pltpu.VMEM((width + STATS, half), f32),
        ],
        in_specs=5,
        flops=heavy,
    )(other, own, *part)
    packed = lax.all_to_all(packed, SPACE, 0, 0, tiled=True)
    tiles = call(combine_space, shape((2 * n_z, rows, width + STATS), bf16), in_specs=1)(packed)
    tiles = lax.all_to_all(tiles, TM, 0, 0, tiled=True)
    whole = pl.BlockSpec(memory_space=pltpu.VMEM)
    parts, middle = call(
        mlp,
        [shape((n_z, 2, rows, width), bf16), shape((rows, width), f32)],
        in_specs=[
            whole,
            pl.BlockSpec((2, 1, rows, width), lambda i, position: (0, position[0], 0, 0)),
            whole,
            whole,
        ],
        prefetch=1,
    )(
        jnp.stack([place, core]).astype(jnp.int32),
        tiles,
        latents.reshape(2, n_space, rows, width),
        up_weight,
        down_weight,
    )
    parts = lax.all_to_all(parts.reshape(2 * n_z, rows, width), TM, 0, 0, tiled=True)
    new = call(finish, shape((n_space, rows, width), bf16), in_specs=2)(parts, middle)
    mine = lax.all_to_all(new, SPACE, 0, 0, tiled=True)
    theirs = lax.ppermute(mine, CORE, [(0, 1), (1, 0)])
    work = [pltpu.VMEM((half, width), bf16), pltpu.VMEM((width, half), bf16)]
    state = [shape((H, count), f32), shape((H, count), f32), shape((width, count), f32)]
    part = call(write_first, state, work, in_specs=2, flops=heavy)(mine, keys)
    new_tokens = call(
        write_second,
        shape((count, width), bf16),
        [*work, pltpu.VMEM((width, count), f32)],
        in_specs=6,
        flops=heavy,
    )(theirs, keys, tokens, *part)
    owned = half * 2 // n_space
    first = place * owned
    source = jnp.where((first >= half) == (core == 1), mine.reshape(half, width), theirs.reshape(half, width))
    new_latents = lax.dynamic_slice_in_dim(source, first % half, owned, 0)
    return (new_tokens, new_latents)


def solution(mesh):
    tm, space = mesh.shape["tm"], mesh.shape["space"]
    split = Mesh(
        mesh.devices.reshape(tm // 2, 2, space // 4, 4), ("tm_0", "tm_1", "space_0", "space_1")
    )
    in_specs = (P(TM_SPACE, None), P(), P(None, TM), P(TM, None))
    out_specs = (P(TM_SPACE, None), P(SPACE, None))
    return jax.shard_map(
        on_device, mesh=split, in_specs=in_specs, out_specs=out_specs, check_vma=False
    )
```

```python
import functools
import math

import jax
import jax.numpy as jnp
from jax import lax
from jax.experimental import pallas as pl
from jax.experimental.pallas import tpu as pltpu
from jax.sharding import Mesh
from jax.sharding import PartitionSpec as P

H = 16
HD = 64
WIDTH = H * HD
Z, CORE = "tm_0", "tm_1"
SPACE = ("space_0", "space_1")
TM = (Z, CORE)
TM_SPACE = TM + SPACE
epsilon = 1e-05
SCALE = HD**-0.5 * math.log2(math.e)
STATS = 128
ONES = 16
SLOTS = 3
CHUNK = 64
f32, bf16 = jnp.float32, jnp.bfloat16


def layer_norm(values):
    center = values - jnp.mean(values, axis=-1, keepdims=True)
    spread = jnp.mean(center * center, axis=-1, keepdims=True)
    return center * lax.rsqrt(spread + epsilon)


def put_values(values_t, values):
    rows = values.shape[0]
    for pair in range(H // 2):
        part = values[:, 2 * HD * pair : 2 * HD * (pair + 1)].T
        for side in range(2):
            values_t[2 * pair + side, :HD, :] = part[side * HD : (side + 1) * HD, :]
    for head in range(H):
        values_t[head, HD:, :] = jnp.ones((ONES, rows), bf16)


def attend(keys, queries, values_t, scores, weights, old_peak, emit):
    peaks = {}

    def score(head):
        pair = slice((head // 2) * 2 * HD, (head // 2 + 1) * 2 * HD)
        query = queries(pair)
        lane = lax.broadcasted_iota(jnp.int32, query.shape, 1)
        query = jnp.where((lane >= HD) == (head % 2 == 1), query, jnp.zeros_like(query))
        found = lax.dot_general(
            keys[:, pair], query, (((1,), (1,)), ((), ())), preferred_element_type=f32
        )
        scores[head % SLOTS] = found
        peak = jnp.max(found, axis=0, keepdims=True) * SCALE
        peaks[head] = peak if old_peak is None else jnp.maximum(peak, old_peak(head))

    def weigh(head):
        peak = jnp.broadcast_to(peaks[head], (CHUNK, peaks[head].shape[1]))
        for at in range(0, scores.shape[1], CHUNK):
            rows = slice(at, at + CHUNK)
            weights[head % SLOTS, rows, :] = jnp.exp2(scores[head % SLOTS, rows, :] * SCALE - peak).astype(bf16)

    def apply(head):
        summed = jnp.dot(values_t[head], weights[head % SLOTS], preferred_element_type=f32)
        emit(head, peaks[head], summed[:HD], summed[HD : HD + 1])

    for step in range(H + 2):
        if step < H:
            score(step)
        if 0 <= step - 1 < H:
            weigh(step - 1)
        if 0 <= step - 2 < H:
            apply(step - 2)


def keep_in(peaks, totals, sums):
    def emit(head, peak, summed, total):
        peaks[head : head + 1, :] = peak
        totals[head : head + 1, :] = total
        sums[head * HD : (head + 1) * HD, :] = summed

    return emit


def joined(peaks, totals, sums, then):
    def emit(head, peak, summed, total):
        old = jnp.exp2(peaks[head : head + 1, :] - peak)
        total = total + totals[head : head + 1, :] * old
        then(head, peak, summed + sums[head * HD : (head + 1) * HD, :] * old, total)

    return emit


def half_of(latents, core, half):
    return lambda pair: latents[pl.ds(pl.multiple_of(core * half, half), half), pair]


def read_first(position, tokens, latents, keys, peaks, totals, sums, values_t, scores, weights):
    value = tokens[...]
    keys[...] = layer_norm(value.astype(f32)).astype(bf16)
    put_values(values_t, value)
    queries = half_of(latents, position[1], latents.shape[0] // 2)
    attend(keys, queries, values_t, scores, weights, None, keep_in(peaks, totals, sums))


def read_second(position, tokens, latents, peaks, totals, sums, packed, keys, values_t, scores, weights, stats):
    value = tokens[...]
    keys[...] = layer_norm(value.astype(f32)).astype(bf16)
    put_values(values_t, value)
    queries = half_of(latents, position[1], latents.shape[0] // 2)
    tiles, rows, _ = packed.shape
    stats[...] = jnp.zeros_like(stats)
    held = {}

    def pack(part):
        return part.T.reshape(tiles, rows, part.shape[0]).astype(bf16)

    def then(head, peak, summed, total):
        sent = peak.astype(bf16).astype(f32)
        scale = jnp.exp2(peak - sent)
        stats[head : head + 1, :] = total * scale
        stats[H + head : H + head + 1, :] = sent
        held[head] = summed * scale
        if head % 2 == 1:
            both = jnp.concatenate([held[head - 1], held[head]], axis=0)
            packed[:, :, (head - 1) * HD : (head + 1) * HD] = pack(both)

    attend(
        keys, queries, values_t, scores, weights,
        lambda head: peaks[head : head + 1, :],
        joined(peaks, totals, sums, then),
    )
    packed[:, :, WIDTH:] = pack(stats[...])


def expand(factor):
    high = factor.astype(bf16)
    rest = factor - high.astype(f32)
    middle = rest.astype(bf16)
    low = (rest - middle.astype(f32)).astype(bf16)
    head = lax.broadcasted_iota(jnp.int32, (3 * H, WIDTH), 0)
    lane = lax.broadcasted_iota(jnp.int32, (3 * H, WIDTH), 1)
    spread = jnp.where(lax.rem(head, H) == lax.div(lane, HD), 1.0, 0.0).astype(bf16)
    return jnp.dot(
        jnp.concatenate([high, middle, low], axis=1), spread, preferred_element_type=f32
    )


def combine(tiles):
    n, rows, _ = tiles.shape
    totals, peaks = tiles[:, :, WIDTH : WIDTH + H], tiles[:, :, WIDTH + H : WIDTH + 2 * H]
    peak = jnp.max(peaks, axis=0)
    factor = jnp.exp2(peaks - peak[None])
    total = jnp.sum(totals * factor, axis=0)
    wide = expand(factor.reshape(n * rows, H)).reshape(n, rows, WIDTH)
    return jnp.sum(tiles[:, :, :WIDTH] * wide, axis=0), total, peak


def combine_space(arrived, out):
    summed, total, peak = combine(arrived[...].astype(f32))
    rest = jnp.zeros((summed.shape[0], STATS - 2 * H), f32)
    tile = jnp.concatenate([summed, total, peak, rest], axis=1).astype(bf16)
    out[...] = jnp.broadcast_to(tile[None], out.shape)


def mlp(position, arrived, latents, up, down, up_other, down_other, out, middle):
    summed, total, _ = combine(arrived[...].astype(f32))
    own = latents[position[1], position[0]].astype(f32)
    middle[...] = own + summed * expand(1.0 / total)
    normed = layer_norm(middle[...]).astype(bf16)
    part = None
    for rise, fall in ((up, down), (up_other, down_other)):
        hidden = jnp.dot(normed, rise[...], preferred_element_type=f32)
        hidden = (0.5 * hidden * (1.0 + lax.erf(hidden * math.sqrt(0.5)))).astype(bf16)
        term = jnp.dot(hidden, fall[...], preferred_element_type=f32)
        part = term if part is None else part + term
    out[...] = jnp.broadcast_to(part.astype(bf16)[None], out.shape)


def finish(parts, middle, out):
    new = (middle[...] + jnp.sum(parts[...].astype(f32), axis=0)).astype(bf16)
    out[...] = jnp.broadcast_to(new[None], out.shape)


def prepare_write(latents, lat, values_t):
    new = latents[...].astype(f32)
    new = new.reshape(new.shape[0] * new.shape[1], new.shape[2])
    lat[...] = new.astype(bf16)
    put_values(values_t, layer_norm(new).astype(bf16))


def write_first(latents, keys, peaks, totals, sums, lat, values_t, scores, weights):
    prepare_write(latents, lat, values_t)
    attend(
        lat, lambda pair: keys[:, pair], values_t, scores, weights, None,
        keep_in(peaks, totals, sums),
    )


def write_second(
    position, latents, mine, keys, tokens, peaks, totals, sums, out, owned, lat, values_t, scores, weights
):
    prepare_write(latents, lat, values_t)
    per = owned.shape[0]
    first = position[0] * per
    tiles = latents.shape[0]
    start = lax.rem(first, tiles)
    theirs = (lax.div(first, tiles) == position[1]).astype(jnp.int32) == 0

    @pl.when(theirs)
    def _():
        owned[...] = latents[pl.ds(start, per)]

    @pl.when(jnp.logical_not(theirs))
    def _():
        owned[...] = mine[pl.ds(start, per)]

    held = {}

    def then(head, peak, summed, total):
        held[head] = summed * (1.0 / total)
        if head % 2 == 1:
            both = jnp.concatenate([held[head - 1], held[head]], axis=0)
            pair = slice((head - 1) * HD, (head + 1) * HD)
            out[:, pair] = (tokens[:, pair].astype(f32) + both.T).astype(bf16)

    attend(
        lat, lambda pair: keys[:, pair], values_t, scores, weights,
        lambda head: peaks[head : head + 1, :],
        joined(peaks, totals, sums, then),
    )


def call(kernel, outs, scratch=(), inputs=1, scalars=False, flops=0):
    whole = pl.BlockSpec(memory_space=pltpu.VMEM)
    single = not isinstance(outs, (list, tuple))
    specs = [whole] * inputs
    if scalars:
        specs = [pl.BlockSpec(memory_space=pltpu.SMEM)] + specs
    return pl.pallas_call(
        kernel,
        out_shape=outs,
        in_specs=specs,
        out_specs=whole if single else [whole] * len(outs),
        scratch_shapes=list(scratch),
        compiler_params=pltpu.CompilerParams(vmem_limit_bytes=48 << 20),
        name=kernel.__name__,
        cost_estimate=pl.CostEstimate(flops=flops, transcendentals=flops // 256, bytes_accessed=1 << 20),
    )


def on_device(tokens, latents, up_weight, down_weight):
    shape = jax.ShapeDtypeStruct
    n_space, n_z = lax.axis_size(SPACE), lax.axis_size(Z)
    count, width = tokens.shape
    half = latents.shape[0] // 2
    rows = half // n_space
    core, place = lax.axis_index(CORE), lax.axis_index(SPACE)
    position = jnp.stack([place, core]).astype(jnp.int32)
    heavy = 4 * half * count * width
    swap = [(0, 1), (1, 0)]

    def work(keys, queries):
        return [
            pltpu.VMEM((H, HD + ONES, keys), bf16),
            pltpu.VMEM((SLOTS, keys, queries), f32),
            pltpu.VMEM((SLOTS, keys, queries), bf16),
        ]

    def state(queries):
        return [shape((H, queries), f32), shape((H, queries), f32), shape((width, queries), f32)]

    other = lax.ppermute(tokens, CORE, swap)
    keys, *part = call(
        read_first, [shape((count, width), bf16), *state(half)], work(count, half),
        inputs=2, scalars=True, flops=heavy,
    )(position, tokens, latents)
    packed = call(
        read_second,
        shape((n_space, rows, width + STATS), bf16),
        [pltpu.VMEM((count, width), bf16), *work(count, half), pltpu.VMEM((STATS, half), f32)],
        inputs=5, scalars=True, flops=heavy,
    )(position, other, latents, *part)
    packed, up_late, down_late = lax.optimization_barrier((packed, up_weight, down_weight))
    packed = lax.all_to_all(packed, SPACE, 0, 0, tiled=True)
    up_other, down_other = lax.ppermute(up_late, CORE, swap), lax.ppermute(down_late, CORE, swap)
    tiles = call(combine_space, shape((n_z, rows, width + STATS), bf16))(packed)
    tiles = lax.all_to_all(tiles, Z, 0, 0, tiled=True)
    parts, middle = call(
        mlp, [shape((n_z, rows, width), bf16), shape((rows, width), f32)], inputs=6, scalars=True
    )(
        position, tiles, latents.reshape(2, n_space, rows, width),
        up_weight, down_weight, up_other, down_other,
    )
    parts = lax.all_to_all(parts, Z, 0, 0, tiled=True)
    new = call(finish, shape((n_space, rows, width), bf16), inputs=2)(parts, middle)
    mine = lax.all_to_all(new, SPACE, 0, 0, tiled=True)
    theirs = lax.ppermute(mine, CORE, swap)
    lat = pltpu.VMEM((half, width), bf16)
    part = call(write_first, state(count), [lat, *work(half, count)], inputs=2, flops=heavy)(mine, keys)
    new_tokens, new_latents = call(
        write_second,
        [shape((count, width), bf16), shape((2, rows, width), bf16)],
        [lat, *work(half, count)],
        inputs=7, scalars=True, flops=heavy,
    )(position, theirs, mine, keys, tokens, *part)
    return (new_tokens, new_latents.reshape(2 * rows, width))


def solution(mesh):
    tm, space = mesh.shape["tm"], mesh.shape["space"]
    split = Mesh(
        mesh.devices.reshape(tm // 2, 2, space // 4, 4), ("tm_0", "tm_1", "space_0", "space_1")
    )
    in_specs = (P(TM_SPACE, None), P(), P(None, TM), P(TM, None))
    out_specs = (P(TM_SPACE, None), P(SPACE, None))
    return jax.shard_map(
        on_device, mesh=split, in_specs=in_specs, out_specs=out_specs, check_vma=False
    )
```

```python
import functools
import math

import jax
import jax.numpy as jnp
from jax import lax
from jax.experimental import pallas as pl
from jax.experimental.pallas import tpu as pltpu
from jax.sharding import Mesh
from jax.sharding import PartitionSpec as P

H = 16
HD = 64
WIDTH = H * HD
Z, CORE = "tm_0", "tm_1"
SPACE = ("space_0", "space_1")
TM = (Z, CORE)
TM_SPACE = TM + SPACE
epsilon = 1e-05
SCALE = HD**-0.5 * math.log2(math.e)
STATS = 128
ONES = 16
SLOTS = 6
CHUNK = 32
SCORE_ROWS = 128
PEAK_ROWS = 32
DELAYS = (0, 2, 3, 5)
LN_ROWS = 16
f32, bf16 = jnp.float32, jnp.bfloat16


def layer_norm(values):
    center = values - jnp.mean(values, axis=-1, keepdims=True)
    spread = jnp.mean(center * center, axis=-1, keepdims=True)
    return center * lax.rsqrt(spread + epsilon)


def put_values(values_t, values):
    rows = values.shape[0]
    for pair in range(H // 2):
        part = values[:, 2 * HD * pair : 2 * HD * (pair + 1)].T
        for side in range(2):
            values_t[2 * pair + side, :HD, :] = part[side * HD : (side + 1) * HD, :]
    for head in range(H):
        values_t[head, HD:, :] = jnp.ones((ONES, rows), bf16)


def place_queries(queries_t, pair, part, at):
    for side in range(2):
        for other in range(2):
            to = slice(at + other * HD, at + (other + 1) * HD)
            mine = part[other * HD : (other + 1) * HD, :]
            queries_t[2 * pair + side, to, :] = mine if other == side else jnp.zeros_like(mine)


def put_queries(queries_t, queries, scaled):
    for pair in range(H // 2):
        part = queries[:, 2 * HD * pair : 2 * HD * (pair + 1)].T
        if scaled:
            exact = part.astype(f32) * SCALE
            high = exact.astype(bf16)
            place_queries(queries_t, pair, high, 0)
            place_queries(queries_t, pair, (exact - high.astype(f32)).astype(bf16), 2 * HD)
        else:
            place_queries(queries_t, pair, part, 0)


def put_normed(normed, tokens, also=None):
    for at in range(0, tokens.shape[0], LN_ROWS):
        rows = slice(at, at + LN_ROWS)
        value = layer_norm(tokens[rows, :].astype(f32)).astype(bf16)
        normed[rows, :] = value
        if also is not None:
            also[rows, :] = value


def attend(keys, queries_t, values_t, scores, weights, old_peak, emit):
    peaks = {}
    scaled = queries_t.shape[1] == 4 * HD

    def scale(values):
        return values if scaled else values * SCALE

    def score(head):
        pair = slice((head // 2) * 2 * HD, (head // 2 + 1) * 2 * HD)
        for at in range(0, scores.shape[1], SCORE_ROWS):
            rows = slice(at, at + SCORE_ROWS)
            left = keys[rows, pair]
            if scaled:
                left = jnp.concatenate([left, left], axis=1)
            scores[head % SLOTS, rows, :] = jnp.dot(left, queries_t[head], preferred_element_type=f32)

    def find_peak(head):
        top = scores[head % SLOTS, :PEAK_ROWS, :]
        for at in range(PEAK_ROWS, scores.shape[1], PEAK_ROWS):
            top = jnp.maximum(top, scores[head % SLOTS, at : at + PEAK_ROWS, :])
        peak = scale(jnp.max(top, axis=0, keepdims=True))
        peaks[head] = peak if old_peak is None else jnp.maximum(peak, old_peak(head))

    def weigh(head):
        peak = jnp.broadcast_to(peaks[head], (CHUNK, peaks[head].shape[1]))
        for at in range(0, scores.shape[1], CHUNK):
            rows = slice(at, at + CHUNK)
            weights[head % SLOTS, rows, :] = jnp.exp2(
                scale(scores[head % SLOTS, rows, :]) - peak
            ).astype(bf16)

    def apply(head):
        summed = jnp.dot(values_t[head], weights[head % SLOTS], preferred_element_type=f32)
        emit(head, peaks[head], summed[:HD], summed[HD : HD + 1])

    stages = (score, find_peak, weigh, apply)
    for step in range(H + DELAYS[-1]):
        for stage, delay in zip(stages, DELAYS):
            if 0 <= step - delay < H:
                stage(step - delay)


def keep_in(peaks, totals, sums):
    def emit(head, peak, summed, total):
        peaks[head : head + 1, :] = peak
        totals[head : head + 1, :] = total
        sums[head * HD : (head + 1) * HD, :] = summed

    return emit


def joined(peaks, totals, sums, then):
    def emit(head, peak, summed, total):
        old = jnp.exp2(peaks[head : head + 1, :] - peak)
        total = total + totals[head : head + 1, :] * old
        then(head, peak, summed + sums[head * HD : (head + 1) * HD, :] * old, total)

    return emit


def read_first(
    position, tokens_hbm, latents_hbm, keys_out, queries_t, peaks, totals, sums,
    tokens, latents, keys, values_t, scores, weights, sems
):
    half = latents.shape[0]
    start = pl.multiple_of(position[1] * half, half)
    get_tokens = pltpu.make_async_copy(tokens_hbm, tokens, sems.at[0])
    get_latents = pltpu.make_async_copy(latents_hbm.at[pl.ds(start, half)], latents, sems.at[1])
    get_tokens.start()
    get_latents.start()
    get_tokens.wait()
    put_normed(keys, tokens, keys_out)
    put_values(values_t, tokens)
    get_latents.wait()
    put_queries(queries_t, latents, False)
    attend(keys, queries_t, values_t, scores, weights, None, keep_in(peaks, totals, sums))


def read_second(tokens, queries_t, peaks, totals, sums, packed, keys, values_t, scores, weights, stats):
    put_normed(keys, tokens)
    put_values(values_t, tokens)
    tiles, rows, _ = packed.shape
    stats[...] = jnp.zeros_like(stats)
    held = {}

    def pack(part):
        return part.T.reshape(tiles, rows, part.shape[0]).astype(bf16)

    def then(head, peak, summed, total):
        sent = peak.astype(bf16).astype(f32)
        scale = jnp.exp2(peak - sent)
        stats[head : head + 1, :] = total * scale
        stats[H + head : H + head + 1, :] = sent
        held[head] = summed * scale
        if head % 2 == 1:
            both = jnp.concatenate([held[head - 1], held[head]], axis=0)
            packed[:, :, (head - 1) * HD : (head + 1) * HD] = pack(both)

    attend(
        keys, queries_t, values_t, scores, weights,
        lambda head: peaks[head : head + 1, :],
        joined(peaks, totals, sums, then),
    )
    packed[:, :, WIDTH:] = pack(stats[...])


def expand(factor):
    high = factor.astype(bf16)
    rest = factor - high.astype(f32)
    middle = rest.astype(bf16)
    low = (rest - middle.astype(f32)).astype(bf16)
    head = lax.broadcasted_iota(jnp.int32, (3 * H, WIDTH), 0)
    lane = lax.broadcasted_iota(jnp.int32, (3 * H, WIDTH), 1)
    spread = jnp.where(lax.rem(head, H) == lax.div(lane, HD), 1.0, 0.0).astype(bf16)
    return jnp.dot(
        jnp.concatenate([high, middle, low], axis=1), spread, preferred_element_type=f32
    )


def combine(tiles):
    n, rows, _ = tiles.shape
    totals, peaks = tiles[:, :, WIDTH : WIDTH + H], tiles[:, :, WIDTH + H : WIDTH + 2 * H]
    peak = jnp.max(peaks, axis=0)
    factor = jnp.exp2(peaks - peak[None])
    total = jnp.sum(totals * factor, axis=0)
    wide = expand(factor.reshape(n * rows, H)).reshape(n, rows, WIDTH)
    return jnp.sum(tiles[:, :, :WIDTH] * wide, axis=0), total, peak


def combine_space(arrived, out):
    summed, total, peak = combine(arrived[...].astype(f32))
    rest = jnp.zeros((summed.shape[0], STATS - 2 * H), f32)
    tile = jnp.concatenate([summed, total, peak, rest], axis=1).astype(bf16)
    out[...] = jnp.broadcast_to(tile[None], out.shape)


def hold(*refs):
    half = len(refs) // 2
    for source, target in zip(refs[:half], refs[half:]):
        target[...] = source[...]


def mlp(arrived, latents, up, down, up_other, down_other, out, middle):
    summed, total, _ = combine(arrived[...].astype(f32))
    own = latents[...].astype(f32)
    middle[...] = own + summed * expand(1.0 / total)
    normed = layer_norm(middle[...]).astype(bf16)
    part = None
    for rise, fall in ((up, down), (up_other, down_other)):
        hidden = jnp.dot(normed, rise[...], preferred_element_type=f32)
        hidden = (0.5 * hidden * (1.0 + lax.erf(hidden * math.sqrt(0.5)))).astype(bf16)
        term = jnp.dot(hidden, fall[...], preferred_element_type=f32)
        part = term if part is None else part + term
    out[...] = jnp.broadcast_to(part.astype(bf16)[None], out.shape)


def finish(parts, middle, out):
    new = (middle[...] + jnp.sum(parts[...].astype(f32), axis=0)).astype(bf16)
    out[...] = jnp.broadcast_to(new[None], out.shape)


def prepare_queries(keys, queries_t):
    put_queries(queries_t, keys, True)


def prepare_write(latents, lat, values, values_t):
    tiles, rows, _ = latents.shape
    for at in range(0, tiles, LN_ROWS // rows):
        new = latents[at : at + LN_ROWS // rows].astype(f32).reshape(LN_ROWS, WIDTH)
        to = slice(at * rows, at * rows + LN_ROWS)
        lat[to, :] = new.astype(bf16)
        values[to, :] = layer_norm(new).astype(bf16)
    put_values(values_t, values)


def write_first(latents, queries_t, peaks, totals, sums, lat, values, values_t, scores, weights):
    prepare_write(latents, lat, values, values_t)
    attend(lat, queries_t, values_t, scores, weights, None, keep_in(peaks, totals, sums))


def write_second(
    position, latents, mine, queries_t, tokens, peaks, totals, sums, out, owned,
    lat, values, values_t, scores, weights
):
    prepare_write(latents, lat, values, values_t)
    per = owned.shape[0]
    first = position[0] * per
    tiles = latents.shape[0]
    start = lax.rem(first, tiles)
    theirs = (lax.div(first, tiles) == position[1]).astype(jnp.int32) == 0

    @pl.when(theirs)
    def _():
        owned[...] = latents[pl.ds(start, per)]

    @pl.when(jnp.logical_not(theirs))
    def _():
        owned[...] = mine[pl.ds(start, per)]

    held = {}

    def then(head, peak, summed, total):
        held[head] = summed * (1.0 / total)
        if head % 2 == 1:
            both = jnp.concatenate([held[head - 1], held[head]], axis=0)
            pair = slice((head - 1) * HD, (head + 1) * HD)
            out[:, pair] = (tokens[:, pair].astype(f32) + both.T).astype(bf16)

    attend(
        lat, queries_t, values_t, scores, weights,
        lambda head: peaks[head : head + 1, :],
        joined(peaks, totals, sums, then),
    )


def call(kernel, outs, scratch=(), inputs=1, scalars=False, flops=0, far=False, limit=16 << 20):
    whole = pl.BlockSpec(memory_space=pltpu.VMEM)
    single = not isinstance(outs, (list, tuple))
    specs = [pl.BlockSpec(memory_space=pltpu.HBM) if far else whole] * inputs
    if scalars:
        specs = [pl.BlockSpec(memory_space=pltpu.SMEM)] + specs
    return pl.pallas_call(
        kernel,
        out_shape=outs,
        in_specs=specs,
        out_specs=whole if single else [whole] * len(outs),
        scratch_shapes=list(scratch),
        compiler_params=pltpu.CompilerParams(vmem_limit_bytes=limit),
        name=kernel.__name__,
        cost_estimate=pl.CostEstimate(flops=flops, transcendentals=flops // 256, bytes_accessed=1 << 20),
    )


def on_device(tokens, latents, up_weight, down_weight):
    shape = jax.ShapeDtypeStruct
    n_space, n_z = lax.axis_size(SPACE), lax.axis_size(Z)
    count, width = tokens.shape
    half = latents.shape[0] // 2
    rows = half // n_space
    core, place = lax.axis_index(CORE), lax.axis_index(SPACE)
    position = jnp.stack([place, core]).astype(jnp.int32)
    heavy = 4 * half * count * width
    swap = [(0, 1), (1, 0)]

    def work(keys, queries):
        return [
            pltpu.VMEM((H, HD + ONES, keys), bf16),
            pltpu.VMEM((SLOTS, keys, queries), f32),
            pltpu.VMEM((SLOTS, keys, queries), bf16),
        ]

    def state(queries):
        return [shape((H, queries), f32), shape((H, queries), f32), shape((width, queries), f32)]

    other = lax.ppermute(tokens, CORE, swap)
    block = lambda rows: pltpu.VMEM((rows, width), bf16)
    keys, queries_t, *part = call(
        read_first,
        [shape((count, width), bf16), shape((H, 2 * HD, half), bf16), *state(half)],
        [block(count), block(half), block(count), *work(count, half), pltpu.SemaphoreType.DMA((2,))],
        inputs=2, scalars=True, flops=heavy, far=True, limit=50 << 20,
    )(position, tokens, latents)
    packed = call(
        read_second,
        shape((n_space, rows, width + STATS), bf16),
        [block(count), *work(count, half), pltpu.VMEM((STATS, half), f32)],
        inputs=5, flops=heavy,
    )(other, queries_t, *part)
    packed, up_late, down_late, keys, late = lax.optimization_barrier(
        (packed, up_weight, down_weight, keys, latents)
    )
    packed = lax.all_to_all(packed, SPACE, 0, 0, tiled=True)
    up_other, down_other = lax.ppermute(up_late, CORE, swap), lax.ppermute(down_late, CORE, swap)
    queries_t = call(
        prepare_queries, shape((H, 4 * HD, count), bf16), flops=1 << 20, limit=60 << 20
    )(keys)
    mine = lax.dynamic_slice_in_dim(late, core * half + place * rows, rows, 0)
    packed, queries_t, up_other, down_other, mine = lax.optimization_barrier(
        (packed, queries_t, up_other, down_other, mine)
    )
    tiles = call(combine_space, shape((n_z, rows, width + STATS), bf16))(packed)
    tiles, *weights = lax.optimization_barrier((tiles, up_late, down_late, up_other, down_other))
    tiles = lax.all_to_all(tiles, Z, 0, 0, tiled=True)
    weights = call(hold, [shape(w.shape, bf16) for w in weights], inputs=4, flops=1 << 20)(*weights)
    tiles, *weights = lax.optimization_barrier((tiles, *weights))
    parts, middle = call(
        mlp, [shape((n_z, rows, width), bf16), shape((rows, width), f32)], inputs=6
    )(tiles, mine, *weights)
    parts = lax.all_to_all(parts, Z, 0, 0, tiled=True)
    new = call(finish, shape((n_space, rows, width), bf16), inputs=2)(parts, middle)
    mine = lax.all_to_all(new, SPACE, 0, 0, tiled=True)
    theirs = lax.ppermute(mine, CORE, swap)
    part = call(
        write_first, state(count), [block(half), block(half), *work(half, count)],
        inputs=2, flops=heavy,
    )(mine, queries_t)
    new_tokens, new_latents = call(
        write_second,
        [shape((count, width), bf16), shape((2, rows, width), bf16)],
        [block(half), block(half), *work(half, count)],
        inputs=7, scalars=True, flops=heavy,
    )(position, theirs, mine, queries_t, tokens, *part)
    return (new_tokens, new_latents.reshape(2 * rows, width))


def solution(mesh):
    tm, space = mesh.shape["tm"], mesh.shape["space"]
    split = Mesh(
        mesh.devices.reshape(tm // 2, 2, space // 4, 4), ("tm_0", "tm_1", "space_0", "space_1")
    )
    in_specs = (P(TM_SPACE, None), P(), P(None, TM), P(TM, None))
    out_specs = (P(TM_SPACE, None), P(SPACE, None))
    return jax.shard_map(
        on_device, mesh=split, in_specs=in_specs, out_specs=out_specs, check_vma=False
    )
```

```python
import functools
import math

import jax
import jax.numpy as jnp
from jax import lax
from jax.experimental import pallas as pl
from jax.experimental.pallas import tpu as pltpu
from jax.sharding import Mesh
from jax.sharding import PartitionSpec as P

H = 16
HD = 64
WIDTH = H * HD
Z, CORE = "tm_0", "tm_1"
SPACE = ("space_0", "space_1")
TM = (Z, CORE)
TM_SPACE = TM + SPACE
epsilon = 1e-05
SCALE = HD**-0.5 * math.log2(math.e)
STATS = 128
ONES = 16
SLOTS = 6
CHUNK = 32
SCORE_ROWS = 128
PEAK_ROWS = 32
DELAYS = (0, 2, 3, 5)
LN_ROWS = 16
f32, bf16 = jnp.float32, jnp.bfloat16


def layer_norm(values):
    center = values - jnp.mean(values, axis=-1, keepdims=True)
    spread = jnp.mean(center * center, axis=-1, keepdims=True)
    return center * lax.rsqrt(spread + epsilon)


def put_values(values_t, values):
    rows = values.shape[0]
    for pair in range(H // 2):
        part = values[:, 2 * HD * pair : 2 * HD * (pair + 1)].T
        for side in range(2):
            values_t[2 * pair + side, :HD, :] = part[side * HD : (side + 1) * HD, :]
    for head in range(H):
        values_t[head, HD:, :] = jnp.ones((ONES, rows), bf16)


def place_queries(queries_t, pair, part, at):
    for side in range(2):
        for other in range(2):
            to = slice(at + other * HD, at + (other + 1) * HD)
            mine = part[other * HD : (other + 1) * HD, :]
            queries_t[2 * pair + side, to, :] = mine if other == side else jnp.zeros_like(mine)


def put_queries(queries_t, queries, scaled):
    for pair in range(H // 2):
        part = queries[:, 2 * HD * pair : 2 * HD * (pair + 1)].T
        if scaled:
            exact = part.astype(f32) * SCALE
            high = exact.astype(bf16)
            place_queries(queries_t, pair, high, 0)
            place_queries(queries_t, pair, (exact - high.astype(f32)).astype(bf16), 2 * HD)
        else:
            place_queries(queries_t, pair, part, 0)


def put_normed(normed, tokens, first, last):
    for at in range(first, last, LN_ROWS):
        rows = slice(at, at + LN_ROWS)
        normed[rows, :] = layer_norm(tokens[rows, :].astype(f32)).astype(bf16)


def attend(keys, queries_t, values_t, scores, weights, old_peak, emit):
    peaks = {}
    scaled = queries_t.shape[1] == 4 * HD

    def scale(values):
        return values if scaled else values * SCALE

    def score(head):
        pair = slice((head // 2) * 2 * HD, (head // 2 + 1) * 2 * HD)
        for at in range(0, scores.shape[1], SCORE_ROWS):
            rows = slice(at, at + SCORE_ROWS)
            left = keys[rows, pair]
            if scaled:
                left = jnp.concatenate([left, left], axis=1)
            scores[head % SLOTS, rows, :] = jnp.dot(left, queries_t[head], preferred_element_type=f32)

    def find_peak(head):
        top = scores[head % SLOTS, :PEAK_ROWS, :]
        for at in range(PEAK_ROWS, scores.shape[1], PEAK_ROWS):
            top = jnp.maximum(top, scores[head % SLOTS, at : at + PEAK_ROWS, :])
        peak = scale(jnp.max(top, axis=0, keepdims=True))
        peaks[head] = peak if old_peak is None else jnp.maximum(peak, old_peak(head))

    def weigh(head):
        peak = jnp.broadcast_to(peaks[head], (CHUNK, peaks[head].shape[1]))
        for at in range(0, scores.shape[1], CHUNK):
            rows = slice(at, at + CHUNK)
            weights[head % SLOTS, rows, :] = jnp.exp2(
                scale(scores[head % SLOTS, rows, :]) - peak
            ).astype(bf16)

    def apply(head):
        summed = jnp.dot(values_t[head], weights[head % SLOTS], preferred_element_type=f32)
        emit(head, peaks[head], summed[:HD], summed[HD : HD + 1])

    stages = (score, find_peak, weigh, apply)
    for step in range(H + DELAYS[-1]):
        for stage, delay in zip(stages, DELAYS):
            if 0 <= step - delay < H:
                stage(step - delay)


def keep_in(peaks, totals, sums):
    def emit(head, peak, summed, total):
        peaks[head : head + 1, :] = peak
        totals[head : head + 1, :] = total
        sums[head * HD : (head + 1) * HD, :] = summed

    return emit


def joined(peaks, totals, sums, then):
    def emit(head, peak, summed, total):
        old = jnp.exp2(peaks[head : head + 1, :] - peak)
        total = total + totals[head : head + 1, :] * old
        then(head, peak, summed + sums[head * HD : (head + 1) * HD, :] * old, total)

    return emit


def prepare_read(
    position, tokens_hbm, latents_hbm, keys, values_t, queries_t, tokens, latents, sems
):
    half, count = latents.shape[0], tokens.shape[0]
    start = position[1] * half
    pieces = sems.shape[0] // 2
    copies = []
    for i in range(pieces):
        size = count // pieces
        rows = pl.ds(i * size, size)
        copies.append(pltpu.make_async_copy(tokens_hbm.at[rows], tokens.at[rows], sems.at[i]))
    for i in range(pieces):
        size = half // pieces
        source = pl.ds(pl.multiple_of(start + i * size, size), size)
        copies.append(
            pltpu.make_async_copy(
                latents_hbm.at[source], latents.at[pl.ds(i * size, size)], sems.at[pieces + i]
            )
        )
    for copy in copies:
        copy.start()
    for i in range(pieces):
        copies[i].wait()
        put_normed(keys, tokens, i * (count // pieces), (i + 1) * (count // pieces))
    put_values(values_t, tokens)
    for copy in copies[pieces:]:
        copy.wait()
    put_queries(queries_t, latents, False)


def read_first(keys, values_t, queries_t, keys_hbm, peaks, totals, sums, scores, weights, sem):
    keep = pltpu.make_async_copy(keys, keys_hbm, sem)
    keep.start()
    attend(keys, queries_t, values_t, scores, weights, None, keep_in(peaks, totals, sums))
    keep.wait()


def read_second(
    tokens, queries_t, peaks, totals, sums, packed_hbm, keys, values_t, scores, weights, stats, packed, sems
):
    put_normed(keys, tokens, 0, tokens.shape[0])
    put_values(values_t, tokens)
    tiles, rows, _ = packed.shape
    stats[...] = jnp.zeros_like(stats)
    held = {}

    copies = []

    def pack(part):
        return part.T.reshape(tiles, rows, part.shape[0]).astype(bf16)

    def send(first, last):
        part = packed.at[:, :, first:last]
        copy = pltpu.make_async_copy(part, packed_hbm.at[:, :, first:last], sems.at[len(copies)])
        copy.start()
        copies.append(copy)

    def then(head, peak, summed, total):
        sent = peak.astype(bf16).astype(f32)
        scale = jnp.exp2(peak - sent)
        stats[head : head + 1, :] = total * scale
        stats[H + head : H + head + 1, :] = sent
        held[head] = summed * scale
        if head % 2 == 1:
            both = jnp.concatenate([held[head - 1], held[head]], axis=0)
            packed[:, :, (head - 1) * HD : (head + 1) * HD] = pack(both)
        if head == H // 2 - 1:
            send(0, WIDTH // 2)

    attend(
        keys, queries_t, values_t, scores, weights,
        lambda head: peaks[head : head + 1, :],
        joined(peaks, totals, sums, then),
    )
    packed[:, :, WIDTH:] = pack(stats[...])
    send(WIDTH // 2, WIDTH + STATS)
    for copy in copies:
        copy.wait()


def expand(factor):
    high = factor.astype(bf16)
    rest = factor - high.astype(f32)
    middle = rest.astype(bf16)
    low = (rest - middle.astype(f32)).astype(bf16)
    head = lax.broadcasted_iota(jnp.int32, (3 * H, WIDTH), 0)
    lane = lax.broadcasted_iota(jnp.int32, (3 * H, WIDTH), 1)
    spread = jnp.where(lax.rem(head, H) == lax.div(lane, HD), 1.0, 0.0).astype(bf16)
    return jnp.dot(
        jnp.concatenate([high, middle, low], axis=1), spread, preferred_element_type=f32
    )


def combine(tiles):
    n, rows, _ = tiles.shape
    totals, peaks = tiles[:, :, WIDTH : WIDTH + H], tiles[:, :, WIDTH + H : WIDTH + 2 * H]
    peak = jnp.max(peaks, axis=0)
    factor = jnp.exp2(peaks - peak[None])
    total = jnp.sum(totals * factor, axis=0)
    wide = expand(factor.reshape(n * rows, H)).reshape(n, rows, WIDTH)
    return jnp.sum(tiles[:, :, :WIDTH] * wide, axis=0), total, peak


def combine_space(arrived, out):
    summed, total, peak = combine(arrived[...].astype(f32))
    rest = jnp.zeros((summed.shape[0], STATS - 2 * H), f32)
    tile = jnp.concatenate([summed, total, peak, rest], axis=1).astype(bf16)
    out[...] = jnp.broadcast_to(tile[None], out.shape)


def hold(*refs):
    *refs, sems = refs
    half = len(refs) // 2
    copies = [
        pltpu.make_async_copy(source, target, sems.at[i])
        for i, (source, target) in enumerate(zip(refs[:half], refs[half:]))
    ]
    for copy in copies:
        copy.start()
    for copy in copies:
        copy.wait()


def mlp(arrived, latents, up, down, up_other, down_other, out, middle):
    summed, total, _ = combine(arrived[...].astype(f32))
    own = latents[...].astype(f32)
    middle[...] = own + summed * expand(1.0 / total)
    normed = layer_norm(middle[...]).astype(bf16)
    part = None
    for rise, fall in ((up, down), (up_other, down_other)):
        hidden = jnp.dot(normed, rise[...], preferred_element_type=f32)
        hidden = (0.5 * hidden * (1.0 + lax.erf(hidden * math.sqrt(0.5)))).astype(bf16)
        term = jnp.dot(hidden, fall[...], preferred_element_type=f32)
        part = term if part is None else part + term
    out[...] = jnp.broadcast_to(part.astype(bf16)[None], out.shape)


def finish(parts, middle, out):
    new = (middle[...] + jnp.sum(parts[...].astype(f32), axis=0)).astype(bf16)
    out[...] = jnp.broadcast_to(new[None], out.shape)


def prepare_queries(keys, queries_t):
    put_queries(queries_t, keys, True)


def prepare_write(latents, lat, values, values_t):
    tiles, rows, _ = latents.shape
    for at in range(0, tiles, LN_ROWS // rows):
        new = latents[at : at + LN_ROWS // rows].astype(f32).reshape(LN_ROWS, WIDTH)
        to = slice(at * rows, at * rows + LN_ROWS)
        lat[to, :] = new.astype(bf16)
        values[to, :] = layer_norm(new).astype(bf16)
    put_values(values_t, values)


def write_first(latents, queries_t, peaks, totals, sums, lat, values, values_t, scores, weights):
    prepare_write(latents, lat, values, values_t)
    attend(lat, queries_t, values_t, scores, weights, None, keep_in(peaks, totals, sums))


def write_second(
    position, latents, mine, queries_t, tokens, peaks, totals, sums, out_hbm, owned,
    lat, values, values_t, scores, weights, out, sems
):
    prepare_write(latents, lat, values, values_t)
    per = owned.shape[0]
    first = position[0] * per
    tiles = latents.shape[0]
    start = lax.rem(first, tiles)
    theirs = (lax.div(first, tiles) == position[1]).astype(jnp.int32) == 0

    @pl.when(theirs)
    def _():
        owned[...] = latents[pl.ds(start, per)]

    @pl.when(jnp.logical_not(theirs))
    def _():
        owned[...] = mine[pl.ds(start, per)]

    held = {}
    copies = []

    def then(head, peak, summed, total):
        held[head] = summed * (1.0 / total)
        if head % 2 == 1:
            both = jnp.concatenate([held[head - 1], held[head]], axis=0)
            pair = slice((head - 1) * HD, (head + 1) * HD)
            out[:, pair] = (tokens[:, pair].astype(f32) + both.T).astype(bf16)
        if head % (H // 2) == H // 2 - 1:
            lanes = slice(head * HD + HD - WIDTH // 2, head * HD + HD)
            copy = pltpu.make_async_copy(
                out.at[:, lanes], out_hbm.at[:, lanes], sems.at[len(copies)]
            )
            copy.start()
            copies.append(copy)

    attend(
        lat, queries_t, values_t, scores, weights,
        lambda head: peaks[head : head + 1, :],
        joined(peaks, totals, sums, then),
    )
    for copy in copies:
        copy.wait()


def call(kernel, outs, scratch=(), inputs=1, scalars=False, flops=0, far=False, far_out=False, limit=16 << 20):
    whole = pl.BlockSpec(memory_space=pltpu.VMEM)
    single = not isinstance(outs, (list, tuple))
    specs = [pl.BlockSpec(memory_space=pltpu.HBM) if far else whole] * inputs
    out_specs = [whole] * (1 if single else len(outs))
    if far_out:
        out_specs[0] = pl.BlockSpec(memory_space=pltpu.HBM)
    if scalars:
        specs = [pl.BlockSpec(memory_space=pltpu.SMEM)] + specs
    return pl.pallas_call(
        kernel,
        out_shape=outs,
        in_specs=specs,
        out_specs=out_specs[0] if single else out_specs,
        scratch_shapes=list(scratch),
        compiler_params=pltpu.CompilerParams(vmem_limit_bytes=limit),
        name=kernel.__name__,
        cost_estimate=pl.CostEstimate(flops=flops, transcendentals=flops // 256, bytes_accessed=1 << 20),
    )


def on_device(tokens, latents, up_weight, down_weight):
    shape = jax.ShapeDtypeStruct
    n_space, n_z = lax.axis_size(SPACE), lax.axis_size(Z)
    count, width = tokens.shape
    half = latents.shape[0] // 2
    rows = half // n_space
    core, place = lax.axis_index(CORE), lax.axis_index(SPACE)
    position = jnp.stack([place, core]).astype(jnp.int32)
    heavy = 4 * half * count * width
    swap = [(0, 1), (1, 0)]

    def work(keys, queries):
        return [
            pltpu.VMEM((H, HD + ONES, keys), bf16),
            pltpu.VMEM((SLOTS, keys, queries), f32),
            pltpu.VMEM((SLOTS, keys, queries), bf16),
        ]

    def state(queries):
        return [shape((H, queries), f32), shape((H, queries), f32), shape((width, queries), f32)]

    block = lambda rows: pltpu.VMEM((rows, width), bf16)
    values, *buffers = work(count, half)
    keys, values_t, queries_t = call(
        prepare_read,
        [
            shape((count, width), bf16), shape((H, HD + ONES, count), bf16),
            shape((H, 2 * HD, half), bf16),
        ],
        [block(count), block(half), pltpu.SemaphoreType.DMA((8,))],
        inputs=2, scalars=True, flops=heavy // 8, far=True, limit=52019 << 10,
    )(position, tokens, latents)
    swapped, keys, values_t, queries_t = lax.optimization_barrier(
        (tokens, keys, values_t, queries_t)
    )
    other = lax.ppermute(swapped, CORE, swap)
    keys, *part = call(
        read_first, [shape((count, width), bf16), *state(half)],
        [*buffers, pltpu.SemaphoreType.DMA],
        inputs=3, flops=heavy, far_out=True, limit=50 << 20,
    )(keys, values_t, queries_t)
    tile = (n_space, rows, width + STATS)
    packed = call(
        read_second, shape(tile, bf16),
        [
            block(count), *work(count, half), pltpu.VMEM((STATS, half), f32), pltpu.VMEM(tile, bf16),
            pltpu.SemaphoreType.DMA((2,)),
        ],
        inputs=5, flops=heavy, far_out=True,
    )(other, queries_t, *part)
    packed, up_late, down_late, keys, late = lax.optimization_barrier(
        (packed, up_weight, down_weight, keys, latents)
    )
    packed = lax.all_to_all(packed, SPACE, 0, 0, tiled=True)
    up_other, down_other = lax.ppermute(up_late, CORE, swap), lax.ppermute(down_late, CORE, swap)
    queries_t = call(
        prepare_queries, shape((H, 4 * HD, count), bf16), flops=1 << 20, limit=60 << 20
    )(keys)
    mine = lax.dynamic_slice_in_dim(late, core * half + place * rows, rows, 0)
    packed, queries_t, up_other, down_other, mine = lax.optimization_barrier(
        (packed, queries_t, up_other, down_other, mine)
    )
    tiles = call(combine_space, shape((n_z, rows, width + STATS), bf16))(packed)
    tiles, *weights = lax.optimization_barrier((tiles, up_late, down_late, up_other, down_other))
    tiles = lax.all_to_all(tiles, Z, 0, 0, tiled=True)
    weights = call(
        hold, [shape(w.shape, bf16) for w in weights], [pltpu.SemaphoreType.DMA((4,))],
        inputs=4, flops=1 << 20, far=True, limit=52838 << 10,
    )(*weights)
    tiles, *weights = lax.optimization_barrier((tiles, *weights))
    parts, middle = call(
        mlp, [shape((n_z, rows, width), bf16), shape((rows, width), f32)], inputs=6
    )(tiles, mine, *weights)
    parts = lax.all_to_all(parts, Z, 0, 0, tiled=True)
    new = call(finish, shape((n_space, rows, width), bf16), inputs=2)(parts, middle)
    mine = lax.all_to_all(new, SPACE, 0, 0, tiled=True)
    theirs = lax.ppermute(mine, CORE, swap)
    part = call(
        write_first, state(count), [block(half), block(half), *work(half, count)],
        inputs=2, flops=heavy,
    )(mine, queries_t)
    new_tokens, new_latents = call(
        write_second,
        [shape((count, width), bf16), shape((2, rows, width), bf16)],
        [
            block(half), block(half), *work(half, count), block(count),
            pltpu.SemaphoreType.DMA((2,)),
        ],
        inputs=7, scalars=True, flops=heavy, far_out=True,
    )(position, theirs, mine, queries_t, tokens, *part)
    return (new_tokens, new_latents.reshape(2 * rows, width))


def solution(mesh):
    tm, space = mesh.shape["tm"], mesh.shape["space"]
    split = Mesh(
        mesh.devices.reshape(tm // 2, 2, space // 4, 4), ("tm_0", "tm_1", "space_0", "space_1")
    )
    in_specs = (P(TM_SPACE, None), P(), P(None, TM), P(TM, None))
    out_specs = (P(TM_SPACE, None), P(SPACE, None))
    return jax.shard_map(
        on_device, mesh=split, in_specs=in_specs, out_specs=out_specs, check_vma=False
    )
```

```python
import functools
import math

import jax
import jax.numpy as jnp
from jax import lax
from jax.experimental import pallas as pl
from jax.experimental.pallas import tpu as pltpu
from jax.sharding import Mesh
from jax.sharding import PartitionSpec as P

H = 16
HD = 64
WIDTH = H * HD
Z, CORE = "tm_0", "tm_1"
SPACE = ("space_0", "space_1")
TM = (Z, CORE)
TM_SPACE = TM + SPACE
epsilon = 1e-05
SCALE = HD**-0.5 * math.log2(math.e)
PARTS = {7: (0, 8), 13: (8, 14), 15: (14, 16)}
STATS = 128
ONES = 16
SLOTS = 6
CHUNK = 32
SCORE_ROWS = 128
PEAK_ROWS = 32
DELAYS = (0, 2, 3, 5)
LN_ROWS = 16
f32, bf16 = jnp.float32, jnp.bfloat16


def layer_norm(values):
    center = values - jnp.mean(values, axis=-1, keepdims=True)
    spread = jnp.mean(center * center, axis=-1, keepdims=True)
    return center * lax.rsqrt(spread + epsilon)


def put_values(values_t, values):
    rows = values.shape[0]
    for pair in range(H // 2):
        part = values[:, 2 * HD * pair : 2 * HD * (pair + 1)].T
        for side in range(2):
            values_t[2 * pair + side, :HD, :] = part[side * HD : (side + 1) * HD, :]
    for head in range(H):
        values_t[head, HD:, :] = jnp.ones((ONES, rows), bf16)


def place_queries(queries_t, pair, part, at):
    for side in range(2):
        for other in range(2):
            to = slice(at + other * HD, at + (other + 1) * HD)
            mine = part[other * HD : (other + 1) * HD, :]
            queries_t[2 * pair + side, to, :] = mine if other == side else jnp.zeros_like(mine)


def put_queries(queries_t, queries, scaled):
    for pair in range(H // 2):
        part = queries[:, 2 * HD * pair : 2 * HD * (pair + 1)].T
        if scaled:
            exact = part.astype(f32) * SCALE
            high = exact.astype(bf16)
            place_queries(queries_t, pair, high, 0)
            place_queries(queries_t, pair, (exact - high.astype(f32)).astype(bf16), 2 * HD)
        else:
            place_queries(queries_t, pair, part, 0)


def put_normed(normed, tokens):
    for at in range(0, tokens.shape[0], LN_ROWS):
        rows = slice(at, at + LN_ROWS)
        normed[rows, :] = layer_norm(tokens[rows, :].astype(f32)).astype(bf16)


def attend(keys, queries_t, values_t, scores, weights, old_peak, emit):
    peaks = {}
    scaled = queries_t.shape[1] == 4 * HD

    def scale(values):
        return values if scaled else values * SCALE

    def score(head):
        pair = slice((head // 2) * 2 * HD, (head // 2 + 1) * 2 * HD)
        for at in range(0, scores.shape[1], SCORE_ROWS):
            rows = slice(at, at + SCORE_ROWS)
            left = keys[rows, pair]
            if scaled:
                left = jnp.concatenate([left, left], axis=1)
            scores[head % SLOTS, rows, :] = jnp.dot(left, queries_t[head], preferred_element_type=f32)

    def find_peak(head):
        top = scores[head % SLOTS, :PEAK_ROWS, :]
        for at in range(PEAK_ROWS, scores.shape[1], PEAK_ROWS):
            top = jnp.maximum(top, scores[head % SLOTS, at : at + PEAK_ROWS, :])
        peak = scale(jnp.max(top, axis=0, keepdims=True))
        peaks[head] = peak if old_peak is None else jnp.maximum(peak, old_peak(head))

    def weigh(head):
        peak = jnp.broadcast_to(peaks[head], (CHUNK, peaks[head].shape[1]))
        for at in range(0, scores.shape[1], CHUNK):
            rows = slice(at, at + CHUNK)
            weights[head % SLOTS, rows, :] = jnp.exp2(
                scale(scores[head % SLOTS, rows, :]) - peak
            ).astype(bf16)

    def apply(head):
        summed = jnp.dot(values_t[head], weights[head % SLOTS], preferred_element_type=f32)
        emit(head, peaks[head], summed[:HD], summed[HD : HD + 1])

    stages = (score, find_peak, weigh, apply)
    for step in range(H + DELAYS[-1]):
        for stage, delay in zip(stages, DELAYS):
            if 0 <= step - delay < H:
                stage(step - delay)


def keep_in(peaks, totals, sums):
    def emit(head, peak, summed, total):
        peaks[head : head + 1, :] = peak
        totals[head : head + 1, :] = total
        sums[head * HD : (head + 1) * HD, :] = summed

    return emit


def joined(peaks, totals, sums, then):
    def emit(head, peak, summed, total):
        old = jnp.exp2(peaks[head : head + 1, :] - peak)
        total = total + totals[head : head + 1, :] * old
        then(head, peak, summed + sums[head * HD : (head + 1) * HD, :] * old, total)

    return emit


def prepare_read(position, latents_hbm, queries_t, latents, sem):
    half = latents.shape[0]
    start = pl.multiple_of(position[1] * half, half)
    get = pltpu.make_async_copy(latents_hbm.at[pl.ds(start, half)], latents, sem)
    get.start()
    get.wait()
    put_queries(queries_t, latents, False)


def read_first(
    tokens, queries_t, keys_hbm, peaks, totals, sums, keys, values_t, scores, weights, sem
):
    put_normed(keys, tokens)
    keep = pltpu.make_async_copy(keys, keys_hbm, sem)
    keep.start()
    put_values(values_t, tokens)
    attend(keys, queries_t, values_t, scores, weights, None, keep_in(peaks, totals, sums))
    keep.wait()


def read_second(
    tokens, queries_t, peaks, totals, sums, packed_hbm, keys, values_t, scores, weights, stats, packed, sems
):
    put_normed(keys, tokens)
    put_values(values_t, tokens)
    tiles, rows, _ = packed.shape
    stats[...] = jnp.zeros_like(stats)
    held = {}

    copies = []

    def pack(part):
        return part.T.reshape(tiles, rows, part.shape[0]).astype(bf16)

    def send(first, last):
        part = packed.at[:, :, first:last]
        copy = pltpu.make_async_copy(part, packed_hbm.at[:, :, first:last], sems.at[len(copies)])
        copy.start()
        copies.append(copy)

    def then(head, peak, summed, total):
        sent = peak.astype(bf16).astype(f32)
        scale = jnp.exp2(peak - sent)
        stats[head : head + 1, :] = total * scale
        stats[H + head : H + head + 1, :] = sent
        held[head] = summed * scale
        if head % 2 == 1:
            both = jnp.concatenate([held[head - 1], held[head]], axis=0)
            packed[:, :, (head - 1) * HD : (head + 1) * HD] = pack(both)
        if head in PARTS and head < H - 1:
            send(PARTS[head][0] * HD, PARTS[head][1] * HD)

    attend(
        keys, queries_t, values_t, scores, weights,
        lambda head: peaks[head : head + 1, :],
        joined(peaks, totals, sums, then),
    )
    packed[:, :, WIDTH:] = pack(stats[...])
    send(PARTS[H - 1][0] * HD, WIDTH + STATS)
    for copy in copies:
        copy.wait()


def expand(factor):
    high = factor.astype(bf16)
    rest = factor - high.astype(f32)
    middle = rest.astype(bf16)
    low = (rest - middle.astype(f32)).astype(bf16)
    head = lax.broadcasted_iota(jnp.int32, (3 * H, WIDTH), 0)
    lane = lax.broadcasted_iota(jnp.int32, (3 * H, WIDTH), 1)
    spread = jnp.where(lax.rem(head, H) == lax.div(lane, HD), 1.0, 0.0).astype(bf16)
    return jnp.dot(
        jnp.concatenate([high, middle, low], axis=1), spread, preferred_element_type=f32
    )


def combine(tiles):
    n, rows, _ = tiles.shape
    totals, peaks = tiles[:, :, WIDTH : WIDTH + H], tiles[:, :, WIDTH + H : WIDTH + 2 * H]
    peak = jnp.max(peaks, axis=0)
    factor = jnp.exp2(peaks - peak[None])
    total = jnp.sum(totals * factor, axis=0)
    wide = expand(factor.reshape(n * rows, H)).reshape(n, rows, WIDTH)
    return jnp.sum(tiles[:, :, :WIDTH] * wide, axis=0), total, peak


def combine_space(arrived, out):
    summed, total, peak = combine(arrived[...].astype(f32))
    rest = jnp.zeros((summed.shape[0], STATS - 2 * H), f32)
    tile = jnp.concatenate([summed, total, peak, rest], axis=1).astype(bf16)
    out[...] = jnp.broadcast_to(tile[None], out.shape)


def hold(*refs):
    *refs, sems = refs
    half = len(refs) // 2
    copies = [
        pltpu.make_async_copy(source, target, sems.at[i])
        for i, (source, target) in enumerate(zip(refs[:half], refs[half:]))
    ]
    for copy in copies:
        copy.start()
    for copy in copies:
        copy.wait()


def mlp(arrived, latents, up, down, up_other, down_other, out, middle):
    summed, total, _ = combine(arrived[...].astype(f32))
    own = latents[...].astype(f32)
    middle[...] = own + summed * expand(1.0 / total)
    normed = layer_norm(middle[...]).astype(bf16)
    part = None
    for rise, fall in ((up, down), (up_other, down_other)):
        hidden = jnp.dot(normed, rise[...], preferred_element_type=f32)
        hidden = (0.5 * hidden * (1.0 + lax.erf(hidden * math.sqrt(0.5)))).astype(bf16)
        term = jnp.dot(hidden, fall[...], preferred_element_type=f32)
        part = term if part is None else part + term
    out[...] = jnp.broadcast_to(part.astype(bf16)[None], out.shape)


def finish(parts, middle, out):
    new = (middle[...] + jnp.sum(parts[...].astype(f32), axis=0)).astype(bf16)
    out[...] = jnp.broadcast_to(new[None], out.shape)


def prepare_queries(keys, queries_t):
    put_queries(queries_t, keys, True)


def prepare_write(latents, lat, values, values_t):
    tiles, rows, _ = latents.shape
    for at in range(0, tiles, LN_ROWS // rows):
        new = latents[at : at + LN_ROWS // rows].astype(f32).reshape(LN_ROWS, WIDTH)
        to = slice(at * rows, at * rows + LN_ROWS)
        lat[to, :] = new.astype(bf16)
        values[to, :] = layer_norm(new).astype(bf16)
    put_values(values_t, values)


def write_first(latents, queries_t, peaks, totals, sums, lat, values, values_t, scores, weights):
    prepare_write(latents, lat, values, values_t)
    attend(lat, queries_t, values_t, scores, weights, None, keep_in(peaks, totals, sums))


def write_second(
    position, latents, mine, queries_t, tokens_hbm, peaks, totals, sums, out_hbm, owned,
    lat, values, values_t, scores, weights, out, tokens, sems
):
    get = pltpu.make_async_copy(tokens_hbm, tokens, sems.at[3])
    get.start()
    prepare_write(latents, lat, values, values_t)
    per = owned.shape[0]
    first = position[0] * per
    tiles = latents.shape[0]
    start = lax.rem(first, tiles)
    theirs = (lax.div(first, tiles) == position[1]).astype(jnp.int32) == 0

    @pl.when(theirs)
    def _():
        owned[...] = latents[pl.ds(start, per)]

    @pl.when(jnp.logical_not(theirs))
    def _():
        owned[...] = mine[pl.ds(start, per)]

    held = {}
    copies = []

    def then(head, peak, summed, total):
        if head == 0:
            get.wait()
        held[head] = summed * (1.0 / total)
        if head % 2 == 1:
            both = jnp.concatenate([held[head - 1], held[head]], axis=0)
            pair = slice((head - 1) * HD, (head + 1) * HD)
            out[:, pair] = (tokens[:, pair].astype(f32) + both.T).astype(bf16)
        if head in PARTS:
            lanes = slice(PARTS[head][0] * HD, PARTS[head][1] * HD)
            copy = pltpu.make_async_copy(
                out.at[:, lanes], out_hbm.at[:, lanes], sems.at[len(copies)]
            )
            copy.start()
            copies.append(copy)

    attend(
        lat, queries_t, values_t, scores, weights,
        lambda head: peaks[head : head + 1, :],
        joined(peaks, totals, sums, then),
    )
    for copy in copies:
        copy.wait()


def call(kernel, outs, scratch=(), inputs=1, scalars=False, flops=0, far=(), far_out=False, limit=16 << 20):
    whole = pl.BlockSpec(memory_space=pltpu.VMEM)
    single = not isinstance(outs, (list, tuple))
    specs = [pl.BlockSpec(memory_space=pltpu.HBM) if i in far else whole for i in range(inputs)]
    out_specs = [whole] * (1 if single else len(outs))
    if far_out:
        out_specs[0] = pl.BlockSpec(memory_space=pltpu.HBM)
    if scalars:
        specs = [pl.BlockSpec(memory_space=pltpu.SMEM)] + specs
    return pl.pallas_call(
        kernel,
        out_shape=outs,
        in_specs=specs,
        out_specs=out_specs[0] if single else out_specs,
        scratch_shapes=list(scratch),
        compiler_params=pltpu.CompilerParams(vmem_limit_bytes=limit),
        name=kernel.__name__,
        cost_estimate=pl.CostEstimate(flops=flops, transcendentals=flops // 256, bytes_accessed=1 << 20),
    )


def on_device(tokens, latents, up_weight, down_weight):
    shape = jax.ShapeDtypeStruct
    n_space, n_z = lax.axis_size(SPACE), lax.axis_size(Z)
    count, width = tokens.shape
    half = latents.shape[0] // 2
    rows = half // n_space
    core, place = lax.axis_index(CORE), lax.axis_index(SPACE)
    position = jnp.stack([place, core]).astype(jnp.int32)
    heavy = 4 * half * count * width
    swap = [(0, 1), (1, 0)]

    def work(keys, queries):
        return [
            pltpu.VMEM((H, HD + ONES, keys), bf16),
            pltpu.VMEM((SLOTS, keys, queries), f32),
            pltpu.VMEM((SLOTS, keys, queries), bf16),
        ]

    def state(queries):
        return [shape((H, queries), f32), shape((H, queries), f32), shape((width, queries), f32)]

    block = lambda rows: pltpu.VMEM((rows, width), bf16)
    queries_t = call(
        prepare_read, shape((H, 2 * HD, half), bf16), [block(half), pltpu.SemaphoreType.DMA],
        inputs=1, scalars=True, flops=heavy // 8, far=(0,), limit=53248 << 10,
    )(position, latents)
    swapped, queries_t = lax.optimization_barrier((tokens, queries_t))
    other = lax.ppermute(swapped, CORE, swap)
    keys, *part = call(
        read_first, [shape((count, width), bf16), *state(half)],
        [block(count), *work(count, half), pltpu.SemaphoreType.DMA],
        inputs=2, flops=heavy, far_out=True,
    )(tokens, queries_t)
    tile = (n_space, rows, width + STATS)
    packed = call(
        read_second, shape(tile, bf16),
        [
            block(count), *work(count, half), pltpu.VMEM((STATS, half), f32), pltpu.VMEM(tile, bf16),
            pltpu.SemaphoreType.DMA((4,)),
        ],
        inputs=5, flops=heavy, far_out=True,
    )(other, queries_t, *part)
    packed, up_late, down_late, keys, late = lax.optimization_barrier(
        (packed, up_weight, down_weight, keys, latents)
    )
    packed = lax.all_to_all(packed, SPACE, 0, 0, tiled=True)
    up_other, down_other = lax.ppermute(up_late, CORE, swap), lax.ppermute(down_late, CORE, swap)
    queries_t = call(
        prepare_queries, shape((H, 4 * HD, count), bf16), flops=1 << 20, limit=53862 << 10
    )(keys)
    mine = lax.dynamic_slice_in_dim(late, core * half + place * rows, rows, 0)
    packed, queries_t, up_other, down_other, mine = lax.optimization_barrier(
        (packed, queries_t, up_other, down_other, mine)
    )
    tiles = call(combine_space, shape((n_z, rows, width + STATS), bf16))(packed)
    tiles, *weights = lax.optimization_barrier((tiles, up_late, down_late, up_other, down_other))
    tiles = lax.all_to_all(tiles, Z, 0, 0, tiled=True)
    weights = call(
        hold, [shape(w.shape, bf16) for w in weights], [pltpu.SemaphoreType.DMA((4,))],
        inputs=4, flops=1 << 20, far=range(4), limit=52838 << 10,
    )(*weights)
    tiles, *weights = lax.optimization_barrier((tiles, *weights))
    parts, middle = call(
        mlp, [shape((n_z, rows, width), bf16), shape((rows, width), f32)], inputs=6
    )(tiles, mine, *weights)
    parts = lax.all_to_all(parts, Z, 0, 0, tiled=True)
    new = call(finish, shape((n_space, rows, width), bf16), inputs=2)(parts, middle)
    mine = lax.all_to_all(new, SPACE, 0, 0, tiled=True)
    theirs = lax.ppermute(mine, CORE, swap)
    part = call(
        write_first, state(count), [block(half), block(half), *work(half, count)],
        inputs=2, flops=heavy,
    )(mine, queries_t)
    new_tokens, new_latents = call(
        write_second,
        [shape((count, width), bf16), shape((2, rows, width), bf16)],
        [
            block(half), block(half), *work(half, count), block(count), block(count),
            pltpu.SemaphoreType.DMA((4,)),
        ],
        inputs=7, scalars=True, flops=heavy, far=(3,), far_out=True,
    )(position, theirs, mine, queries_t, tokens, *part)
    return (new_tokens, new_latents.reshape(2 * rows, width))


def solution(mesh):
    tm, space = mesh.shape["tm"], mesh.shape["space"]
    split = Mesh(
        mesh.devices.reshape(tm // 2, 2, space // 4, 4), ("tm_0", "tm_1", "space_0", "space_1")
    )
    in_specs = (P(TM_SPACE, None), P(), P(None, TM), P(TM, None))
    out_specs = (P(TM_SPACE, None), P(SPACE, None))
    return jax.shard_map(
        on_device, mesh=split, in_specs=in_specs, out_specs=out_specs, check_vma=False
    )
```

```python
import functools
import math

import jax
import jax.numpy as jnp
from jax import lax
from jax.experimental import pallas as pl
from jax.experimental.pallas import tpu as pltpu
from jax.sharding import Mesh
from jax.sharding import PartitionSpec as P

H = 16
HD = 64
WIDTH = H * HD
Z, CORE = "tm_0", "tm_1"
SPACE = ("space_0", "space_1")
TM = (Z, CORE)
TM_SPACE = TM + SPACE
epsilon = 1e-05
SCALE = HD**-0.5 * math.log2(math.e)
PARTS = {7: (0, 8), 13: (8, 14), 15: (14, 16)}
STATS = 128
ONES = 16
SLOTS = 6
CHUNK = 32
SCORE_ROWS = 128
PEAK_ROWS = 32
DELAYS = (0, 2, 3, 5)
LN_ROWS = 16
f32, bf16 = jnp.float32, jnp.bfloat16


def layer_norm(values):
    center = values - jnp.mean(values, axis=-1, keepdims=True)
    spread = jnp.mean(center * center, axis=-1, keepdims=True)
    return center * lax.rsqrt(spread + epsilon)


def put_values(values_t, values):
    rows = values.shape[0]
    for pair in range(H // 2):
        part = values[:, 2 * HD * pair : 2 * HD * (pair + 1)].T
        for side in range(2):
            values_t[2 * pair + side, :HD, :] = part[side * HD : (side + 1) * HD, :]
    for head in range(H):
        values_t[head, HD:, :] = jnp.ones((ONES, rows), bf16)


def place_queries(queries_t, pair, part, at):
    for side in range(2):
        for other in range(2):
            to = slice(at + other * HD, at + (other + 1) * HD)
            mine = part[other * HD : (other + 1) * HD, :]
            queries_t[2 * pair + side, to, :] = mine if other == side else jnp.zeros_like(mine)


def put_queries(queries_t, queries, scaled):
    for pair in range(H // 2):
        part = queries[:, 2 * HD * pair : 2 * HD * (pair + 1)].T
        if scaled:
            exact = part.astype(f32) * SCALE
            high = exact.astype(bf16)
            place_queries(queries_t, pair, high, 0)
            place_queries(queries_t, pair, (exact - high.astype(f32)).astype(bf16), 2 * HD)
        else:
            place_queries(queries_t, pair, part, 0)


def put_normed(normed, tokens):
    for at in range(0, tokens.shape[0], LN_ROWS):
        rows = slice(at, at + LN_ROWS)
        normed[rows, :] = layer_norm(tokens[rows, :].astype(f32)).astype(bf16)


def attend(keys, queries_t, values_t, scores, weights, old_peak, emit):
    peaks = {}
    scaled = queries_t.shape[1] == 4 * HD

    def scale(values):
        return values if scaled else values * SCALE

    def score(head):
        pair = slice((head // 2) * 2 * HD, (head // 2 + 1) * 2 * HD)
        for at in range(0, scores.shape[1], SCORE_ROWS):
            rows = slice(at, at + SCORE_ROWS)
            left = keys[rows, pair]
            if scaled:
                left = jnp.concatenate([left, left], axis=1)
            scores[head % SLOTS, rows, :] = jnp.dot(left, queries_t[head], preferred_element_type=f32)

    def find_peak(head):
        top = scores[head % SLOTS, :PEAK_ROWS, :]
        for at in range(PEAK_ROWS, scores.shape[1], PEAK_ROWS):
            top = jnp.maximum(top, scores[head % SLOTS, at : at + PEAK_ROWS, :])
        peak = scale(jnp.max(top, axis=0, keepdims=True))
        peaks[head] = peak if old_peak is None else jnp.maximum(peak, old_peak(head))

    def weigh(head):
        peak = jnp.broadcast_to(peaks[head], (CHUNK, peaks[head].shape[1]))
        for at in range(0, scores.shape[1], CHUNK):
            rows = slice(at, at + CHUNK)
            weights[head % SLOTS, rows, :] = jnp.exp2(
                scale(scores[head % SLOTS, rows, :]) - peak
            ).astype(bf16)

    def apply(head):
        summed = jnp.dot(values_t[head], weights[head % SLOTS], preferred_element_type=f32)
        emit(head, peaks[head], summed[:HD], summed[HD : HD + 1])

    stages = (score, find_peak, weigh, apply)
    for step in range(H + DELAYS[-1]):
        for stage, delay in zip(stages, DELAYS):
            if 0 <= step - delay < H:
                stage(step - delay)


def keep_in(peaks, totals, sums):
    def emit(head, peak, summed, total):
        peaks[head : head + 1, :] = peak
        totals[head : head + 1, :] = total
        sums[head * HD : (head + 1) * HD, :] = summed

    return emit


def joined(peaks, totals, sums, then):
    def emit(head, peak, summed, total):
        old = jnp.exp2(peaks[head : head + 1, :] - peak)
        total = total + totals[head : head + 1, :] * old
        then(head, peak, summed + sums[head * HD : (head + 1) * HD, :] * old, total)

    return emit


def prepare_read(position, latents_hbm, queries_t, latents, sem):
    half = latents.shape[0]
    start = pl.multiple_of(position[1] * half, half)
    get = pltpu.make_async_copy(latents_hbm.at[pl.ds(start, half)], latents, sem)
    get.start()
    get.wait()
    put_queries(queries_t, latents, False)


def read_first(
    tokens, queries_t, keys_hbm, peaks, totals, sums, keys, values_t, scores, weights, sem
):
    put_normed(keys, tokens)
    keep = pltpu.make_async_copy(keys, keys_hbm, sem)
    keep.start()
    put_values(values_t, tokens)
    attend(keys, queries_t, values_t, scores, weights, None, keep_in(peaks, totals, sums))
    keep.wait()


def read_second(
    tokens, queries_t, peaks, totals, sums, packed_hbm, keys, values_t, scores, weights, stats, packed, sems
):
    put_normed(keys, tokens)
    put_values(values_t, tokens)
    tiles, rows, _ = packed.shape
    stats[...] = jnp.zeros_like(stats)
    held = {}

    copies = []

    def pack(part):
        return part.T.reshape(tiles, rows, part.shape[0]).astype(bf16)

    def send(first, last):
        part = packed.at[:, :, first:last]
        copy = pltpu.make_async_copy(part, packed_hbm.at[:, :, first:last], sems.at[len(copies)])
        copy.start()
        copies.append(copy)

    def then(head, peak, summed, total):
        sent = peak.astype(bf16).astype(f32)
        scale = jnp.exp2(peak - sent)
        stats[head : head + 1, :] = total * scale
        stats[H + head : H + head + 1, :] = sent
        held[head] = summed * scale
        if head % 2 == 1:
            both = jnp.concatenate([held[head - 1], held[head]], axis=0)
            packed[:, :, (head - 1) * HD : (head + 1) * HD] = pack(both)
        if head in PARTS and head < H - 1:
            send(PARTS[head][0] * HD, PARTS[head][1] * HD)

    attend(
        keys, queries_t, values_t, scores, weights,
        lambda head: peaks[head : head + 1, :],
        joined(peaks, totals, sums, then),
    )
    packed[:, :, WIDTH:] = pack(stats[...])
    send(PARTS[H - 1][0] * HD, WIDTH + STATS)
    for copy in copies:
        copy.wait()


def expand(factor):
    high = factor.astype(bf16)
    rest = factor - high.astype(f32)
    middle = rest.astype(bf16)
    low = (rest - middle.astype(f32)).astype(bf16)
    head = lax.broadcasted_iota(jnp.int32, (3 * H, WIDTH), 0)
    lane = lax.broadcasted_iota(jnp.int32, (3 * H, WIDTH), 1)
    spread = jnp.where(lax.rem(head, H) == lax.div(lane, HD), 1.0, 0.0).astype(bf16)
    return jnp.dot(
        jnp.concatenate([high, middle, low], axis=1), spread, preferred_element_type=f32
    )


def combine(tiles):
    n, rows, _ = tiles.shape
    totals, peaks = tiles[:, :, WIDTH : WIDTH + H], tiles[:, :, WIDTH + H : WIDTH + 2 * H]
    peak = jnp.max(peaks, axis=0)
    factor = jnp.exp2(peaks - peak[None])
    total = jnp.sum(totals * factor, axis=0)
    wide = expand(factor.reshape(n * rows, H)).reshape(n, rows, WIDTH)
    return jnp.sum(tiles[:, :, :WIDTH] * wide, axis=0), total, peak


def combine_space(arrived, out):
    summed, total, peak = combine(arrived[...].astype(f32))
    rest = jnp.zeros((summed.shape[0], STATS - 2 * H), f32)
    tile = jnp.concatenate([summed, total, peak, rest], axis=1).astype(bf16)
    out[...] = jnp.broadcast_to(tile[None], out.shape)


def hold(*refs):
    *refs, sems = refs
    half = len(refs) // 2
    copies = [
        pltpu.make_async_copy(source, target, sems.at[i])
        for i, (source, target) in enumerate(zip(refs[:half], refs[half:]))
    ]
    for copy in copies:
        copy.start()
    for copy in copies:
        copy.wait()


def mlp(arrived, latents, up, down, up_other, down_other, out, middle):
    summed, total, _ = combine(arrived[...].astype(f32))
    own = latents[...].astype(f32)
    middle[...] = own + summed * expand(1.0 / total)
    normed = layer_norm(middle[...]).astype(bf16)
    part = None
    for rise, fall in ((up, down), (up_other, down_other)):
        hidden = jnp.dot(normed, rise[...], preferred_element_type=f32)
        hidden = (0.5 * hidden * (1.0 + lax.erf(hidden * math.sqrt(0.5)))).astype(bf16)
        term = jnp.dot(hidden, fall[...], preferred_element_type=f32)
        part = term if part is None else part + term
    out[...] = jnp.broadcast_to(part.astype(bf16)[None], out.shape)


def finish(parts, middle, out):
    new = (middle[...] + jnp.sum(parts[...].astype(f32), axis=0)).astype(bf16)
    out[...] = jnp.broadcast_to(new[None], out.shape)


def prepare_queries(keys, queries_t):
    put_queries(queries_t, keys, True)


def prepare_write(latents, lat, values, values_t):
    tiles, rows, _ = latents.shape
    for at in range(0, tiles, LN_ROWS // rows):
        new = latents[at : at + LN_ROWS // rows].astype(f32).reshape(LN_ROWS, WIDTH)
        to = slice(at * rows, at * rows + LN_ROWS)
        lat[to, :] = new.astype(bf16)
        values[to, :] = layer_norm(new).astype(bf16)
    put_values(values_t, values)


def write_first(
    latents, queries_t, tokens_hbm, peaks, totals, sums, tokens, lat, values, values_t, scores, weights, sem
):
    get = pltpu.make_async_copy(tokens_hbm, tokens, sem)
    get.start()
    prepare_write(latents, lat, values, values_t)
    attend(lat, queries_t, values_t, scores, weights, None, keep_in(peaks, totals, sums))
    get.wait()


def write_second(
    position, latents, mine, queries_t, tokens, peaks, totals, sums, out, owned,
    lat, values, values_t, scores, weights
):
    prepare_write(latents, lat, values, values_t)
    per = owned.shape[0]
    first = position[0] * per
    tiles = latents.shape[0]
    start = lax.rem(first, tiles)
    theirs = (lax.div(first, tiles) == position[1]).astype(jnp.int32) == 0

    @pl.when(theirs)
    def _():
        owned[...] = latents[pl.ds(start, per)]

    @pl.when(jnp.logical_not(theirs))
    def _():
        owned[...] = mine[pl.ds(start, per)]

    held = {}

    def then(head, peak, summed, total):
        held[head] = summed * (1.0 / total)
        if head % 2 == 1:
            both = jnp.concatenate([held[head - 1], held[head]], axis=0)
            pair = slice((head - 1) * HD, (head + 1) * HD)
            out[:, pair] = (tokens[:, pair].astype(f32) + both.T).astype(bf16)

    attend(
        lat, queries_t, values_t, scores, weights,
        lambda head: peaks[head : head + 1, :],
        joined(peaks, totals, sums, then),
    )


def call(kernel, outs, scratch=(), inputs=1, scalars=False, flops=0, far=(), far_out=False, limit=16 << 20):
    whole = pl.BlockSpec(memory_space=pltpu.VMEM)
    single = not isinstance(outs, (list, tuple))
    specs = [pl.BlockSpec(memory_space=pltpu.HBM) if i in far else whole for i in range(inputs)]
    out_specs = [whole] * (1 if single else len(outs))
    if far_out:
        out_specs[0] = pl.BlockSpec(memory_space=pltpu.HBM)
    if scalars:
        specs = [pl.BlockSpec(memory_space=pltpu.SMEM)] + specs
    return pl.pallas_call(
        kernel,
        out_shape=outs,
        in_specs=specs,
        out_specs=out_specs[0] if single else out_specs,
        scratch_shapes=list(scratch),
        compiler_params=pltpu.CompilerParams(vmem_limit_bytes=limit),
        name=kernel.__name__,
        cost_estimate=pl.CostEstimate(flops=flops, transcendentals=flops // 256, bytes_accessed=1 << 20),
    )


def on_device(tokens, latents, up_weight, down_weight):
    shape = jax.ShapeDtypeStruct
    n_space, n_z = lax.axis_size(SPACE), lax.axis_size(Z)
    count, width = tokens.shape
    half = latents.shape[0] // 2
    rows = half // n_space
    core, place = lax.axis_index(CORE), lax.axis_index(SPACE)
    position = jnp.stack([place, core]).astype(jnp.int32)
    heavy = 4 * half * count * width
    swap = [(0, 1), (1, 0)]

    def work(keys, queries):
        return [
            pltpu.VMEM((H, HD + ONES, keys), bf16),
            pltpu.VMEM((SLOTS, keys, queries), f32),
            pltpu.VMEM((SLOTS, keys, queries), bf16),
        ]

    def state(queries):
        return [shape((H, queries), f32), shape((H, queries), f32), shape((width, queries), f32)]

    block = lambda rows: pltpu.VMEM((rows, width), bf16)
    queries_t = call(
        prepare_read, shape((H, 2 * HD, half), bf16), [block(half), pltpu.SemaphoreType.DMA],
        inputs=1, scalars=True, flops=heavy // 8, far=(0,), limit=53248 << 10,
    )(position, latents)
    swapped, queries_t = lax.optimization_barrier((tokens, queries_t))
    other = lax.ppermute(swapped, CORE, swap)
    keys, *part = call(
        read_first, [shape((count, width), bf16), *state(half)],
        [block(count), *work(count, half), pltpu.SemaphoreType.DMA],
        inputs=2, flops=heavy, far_out=True,
    )(tokens, queries_t)
    tile = (n_space, rows, width + STATS)
    packed = call(
        read_second, shape(tile, bf16),
        [
            block(count), *work(count, half), pltpu.VMEM((STATS, half), f32), pltpu.VMEM(tile, bf16),
            pltpu.SemaphoreType.DMA((3,)),
        ],
        inputs=5, flops=heavy, far_out=True,
    )(other, queries_t, *part)
    packed, up_late, down_late, keys, late = lax.optimization_barrier(
        (packed, up_weight, down_weight, keys, latents)
    )
    packed = lax.all_to_all(packed, SPACE, 0, 0, tiled=True)
    up_other, down_other = lax.ppermute(up_late, CORE, swap), lax.ppermute(down_late, CORE, swap)
    queries_t = call(
        prepare_queries, shape((H, 4 * HD, count), bf16), flops=1 << 20, limit=53862 << 10
    )(keys)
    mine = lax.dynamic_slice_in_dim(late, core * half + place * rows, rows, 0)
    packed, queries_t, up_other, down_other, mine = lax.optimization_barrier(
        (packed, queries_t, up_other, down_other, mine)
    )
    tiles = call(combine_space, shape((n_z, rows, width + STATS), bf16))(packed)
    tiles, *weights = lax.optimization_barrier((tiles, up_late, down_late, up_other, down_other))
    tiles = lax.all_to_all(tiles, Z, 0, 0, tiled=True)
    weights = call(
        hold, [shape(w.shape, bf16) for w in weights], [pltpu.SemaphoreType.DMA((4,))],
        inputs=4, flops=1 << 20, far=range(4), limit=52838 << 10,
    )(*weights)
    tiles, *weights = lax.optimization_barrier((tiles, *weights))
    parts, middle = call(
        mlp, [shape((n_z, rows, width), bf16), shape((rows, width), f32)], inputs=6
    )(tiles, mine, *weights)
    parts = lax.all_to_all(parts, Z, 0, 0, tiled=True)
    new = call(finish, shape((n_space, rows, width), bf16), inputs=2)(parts, middle)
    mine = lax.all_to_all(new, SPACE, 0, 0, tiled=True)
    theirs = lax.ppermute(mine, CORE, swap)
    *part, held = call(
        write_first, [*state(count), shape((count, width), bf16)],
        [block(half), block(half), *work(half, count), pltpu.SemaphoreType.DMA],
        inputs=3, flops=heavy, far=(2,),
    )(mine, queries_t, tokens)
    new_tokens, new_latents = call(
        write_second,
        [shape((count, width), bf16), shape((2, rows, width), bf16)],
        [block(half), block(half), *work(half, count)],
        inputs=7, scalars=True, flops=heavy,
    )(position, theirs, mine, queries_t, held, *part)
    return (new_tokens, new_latents.reshape(2 * rows, width))


def solution(mesh):
    tm, space = mesh.shape["tm"], mesh.shape["space"]
    split = Mesh(
        mesh.devices.reshape(tm // 2, 2, space // 4, 4), ("tm_0", "tm_1", "space_0", "space_1")
    )
    in_specs = (P(TM_SPACE, None), P(), P(None, TM), P(TM, None))
    out_specs = (P(TM_SPACE, None), P(SPACE, None))
    return jax.shard_map(
        on_device, mesh=split, in_specs=in_specs, out_specs=out_specs, check_vma=False
    )
```

```python
import functools
import math

import jax
import jax.numpy as jnp
from jax import lax
from jax.experimental import pallas as pl
from jax.experimental.pallas import tpu as pltpu
from jax.sharding import Mesh
from jax.sharding import PartitionSpec as P

H = 16
HD = 64
WIDTH = H * HD
Z, CORE = "tm_0", "tm_1"
SPACE = ("space_0", "space_1")
TM = (Z, CORE)
TM_SPACE = TM + SPACE
epsilon = 1e-05
SCALE = HD**-0.5 * math.log2(math.e)
PARTS = {7: (0, 8), 13: (8, 14), 15: (14, 16)}
STATS = 128
ONES = 16
SLOTS = 6
CHUNK = 32
SCORE_ROWS = 128
PEAK_ROWS = 32
DELAYS = (0, 2, 3, 5)
LN_ROWS = 16
f32, bf16 = jnp.float32, jnp.bfloat16


def layer_norm(values):
    center = values - jnp.mean(values, axis=-1, keepdims=True)
    spread = jnp.mean(center * center, axis=-1, keepdims=True)
    return center * lax.rsqrt(spread + epsilon)


def put_values(values_t, values):
    rows = values.shape[0]
    for pair in range(H // 2):
        part = values[:, 2 * HD * pair : 2 * HD * (pair + 1)].T
        for side in range(2):
            values_t[2 * pair + side, :HD, :] = part[side * HD : (side + 1) * HD, :]
    for head in range(H):
        values_t[head, HD:, :] = jnp.ones((ONES, rows), bf16)


def place_queries(queries_t, pair, part, at):
    for side in range(2):
        for other in range(2):
            to = slice(at + other * HD, at + (other + 1) * HD)
            mine = part[other * HD : (other + 1) * HD, :]
            queries_t[2 * pair + side, to, :] = mine if other == side else jnp.zeros_like(mine)


def put_queries(queries_t, queries, scaled):
    for pair in range(H // 2):
        part = queries[:, 2 * HD * pair : 2 * HD * (pair + 1)].T
        if scaled:
            exact = part.astype(f32) * SCALE
            high = exact.astype(bf16)
            place_queries(queries_t, pair, high, 0)
            place_queries(queries_t, pair, (exact - high.astype(f32)).astype(bf16), 2 * HD)
        else:
            place_queries(queries_t, pair, part, 0)


def put_normed(normed, tokens):
    for at in range(0, tokens.shape[0], LN_ROWS):
        rows = slice(at, at + LN_ROWS)
        normed[rows, :] = layer_norm(tokens[rows, :].astype(f32)).astype(bf16)


def attend(keys, queries_t, values_t, scores, weights, old_peak, emit):
    peaks = {}
    scaled = queries_t.shape[1] == 4 * HD

    def scale(values):
        return values if scaled else values * SCALE

    def score(head):
        pair = slice((head // 2) * 2 * HD, (head // 2 + 1) * 2 * HD)
        for at in range(0, scores.shape[1], SCORE_ROWS):
            rows = slice(at, at + SCORE_ROWS)
            left = keys[rows, pair]
            if scaled:
                left = jnp.concatenate([left, left], axis=1)
            scores[head % SLOTS, rows, :] = jnp.dot(left, queries_t[head], preferred_element_type=f32)

    def find_peak(head):
        top = scores[head % SLOTS, :PEAK_ROWS, :]
        for at in range(PEAK_ROWS, scores.shape[1], PEAK_ROWS):
            top = jnp.maximum(top, scores[head % SLOTS, at : at + PEAK_ROWS, :])
        peak = scale(jnp.max(top, axis=0, keepdims=True))
        peaks[head] = peak if old_peak is None else jnp.maximum(peak, old_peak(head))

    def weigh(head):
        peak = jnp.broadcast_to(peaks[head], (CHUNK, peaks[head].shape[1]))
        for at in range(0, scores.shape[1], CHUNK):
            rows = slice(at, at + CHUNK)
            weights[head % SLOTS, rows, :] = jnp.exp2(
                scale(scores[head % SLOTS, rows, :]) - peak
            ).astype(bf16)

    def apply(head):
        summed = jnp.dot(values_t[head], weights[head % SLOTS], preferred_element_type=f32)
        emit(head, peaks[head], summed[:HD], summed[HD : HD + 1])

    stages = (score, find_peak, weigh, apply)
    for step in range(H + DELAYS[-1]):
        for stage, delay in zip(stages, DELAYS):
            if 0 <= step - delay < H:
                stage(step - delay)


def keep_in(peaks, totals, sums):
    def emit(head, peak, summed, total):
        peaks[head : head + 1, :] = peak
        totals[head : head + 1, :] = total
        sums[head * HD : (head + 1) * HD, :] = summed

    return emit


def joined(peaks, totals, sums, then):
    def emit(head, peak, summed, total):
        old = jnp.exp2(peaks[head : head + 1, :] - peak)
        total = total + totals[head : head + 1, :] * old
        then(head, peak, summed + sums[head * HD : (head + 1) * HD, :] * old, total)

    return emit


def prepare_read(position, latents_hbm, queries_t, latents, sem):
    half = latents.shape[0]
    start = pl.multiple_of(position[1] * half, half)
    get = pltpu.make_async_copy(latents_hbm.at[pl.ds(start, half)], latents, sem)
    get.start()
    get.wait()
    put_queries(queries_t, latents, False)


def read_first(
    tokens, queries_t, keys_hbm, peaks, totals, sums, keys, values_t, scores, weights, sem
):
    put_normed(keys, tokens)
    keep = pltpu.make_async_copy(keys, keys_hbm, sem)
    keep.start()
    put_values(values_t, tokens)
    attend(keys, queries_t, values_t, scores, weights, None, keep_in(peaks, totals, sums))
    keep.wait()


def read_second(
    tokens, queries_t, peaks, totals, sums, packed_hbm, keys, values_t, scores, weights, stats, packed, sems
):
    put_normed(keys, tokens)
    put_values(values_t, tokens)
    tiles, rows, _ = packed.shape
    stats[...] = jnp.zeros_like(stats)
    held = {}

    copies = []

    def pack(part):
        return part.T.reshape(tiles, rows, part.shape[0]).astype(bf16)

    def send(first, last):
        part = packed.at[:, :, first:last]
        copy = pltpu.make_async_copy(part, packed_hbm.at[:, :, first:last], sems.at[len(copies)])
        copy.start()
        copies.append(copy)

    def then(head, peak, summed, total):
        sent = peak.astype(bf16).astype(f32)
        scale = jnp.exp2(peak - sent)
        stats[head : head + 1, :] = total * scale
        stats[H + head : H + head + 1, :] = sent
        held[head] = summed * scale
        if head % 2 == 1:
            both = jnp.concatenate([held[head - 1], held[head]], axis=0)
            packed[:, :, (head - 1) * HD : (head + 1) * HD] = pack(both)
        if head in PARTS and head < H - 1:
            send(PARTS[head][0] * HD, PARTS[head][1] * HD)

    attend(
        keys, queries_t, values_t, scores, weights,
        lambda head: peaks[head : head + 1, :],
        joined(peaks, totals, sums, then),
    )
    packed[:, :, WIDTH:] = pack(stats[...])
    send(PARTS[H - 1][0] * HD, WIDTH + STATS)
    for copy in copies:
        copy.wait()


def expand(factor):
    high = factor.astype(bf16)
    rest = factor - high.astype(f32)
    middle = rest.astype(bf16)
    low = (rest - middle.astype(f32)).astype(bf16)
    head = lax.broadcasted_iota(jnp.int32, (3 * H, WIDTH), 0)
    lane = lax.broadcasted_iota(jnp.int32, (3 * H, WIDTH), 1)
    spread = jnp.where(lax.rem(head, H) == lax.div(lane, HD), 1.0, 0.0).astype(bf16)
    return jnp.dot(
        jnp.concatenate([high, middle, low], axis=1), spread, preferred_element_type=f32
    )


def combine(tiles):
    n, rows, _ = tiles.shape
    totals, peaks = tiles[:, :, WIDTH : WIDTH + H], tiles[:, :, WIDTH + H : WIDTH + 2 * H]
    peak = jnp.max(peaks, axis=0)
    factor = jnp.exp2(peaks - peak[None])
    total = jnp.sum(totals * factor, axis=0)
    wide = expand(factor.reshape(n * rows, H)).reshape(n, rows, WIDTH)
    return jnp.sum(tiles[:, :, :WIDTH] * wide, axis=0), total, peak


def combine_space(arrived, out):
    summed, total, peak = combine(arrived[...].astype(f32))
    rest = jnp.zeros((summed.shape[0], STATS - 2 * H), f32)
    tile = jnp.concatenate([summed, total, peak, rest], axis=1).astype(bf16)
    out[...] = jnp.broadcast_to(tile[None], out.shape)


def hold(*refs):
    *refs, sems = refs
    half = len(refs) // 2
    copies = [
        pltpu.make_async_copy(source, target, sems.at[i])
        for i, (source, target) in enumerate(zip(refs[:half], refs[half:]))
    ]
    for copy in copies:
        copy.start()
    for copy in copies:
        copy.wait()


def mlp(arrived, latents, up, down, up_other, down_other, out, middle):
    summed, total, _ = combine(arrived[...].astype(f32))
    own = latents[...].astype(f32)
    middle[...] = own + summed * expand(1.0 / total)
    normed = layer_norm(middle[...]).astype(bf16)
    part = None
    for rise, fall in ((up, down), (up_other, down_other)):
        hidden = jnp.dot(normed, rise[...], preferred_element_type=f32)
        hidden = (0.5 * hidden * (1.0 + lax.erf(hidden * math.sqrt(0.5)))).astype(bf16)
        term = jnp.dot(hidden, fall[...], preferred_element_type=f32)
        part = term if part is None else part + term
    out[...] = jnp.broadcast_to(part.astype(bf16)[None], out.shape)


def finish(parts, middle, out):
    new = (middle[...] + jnp.sum(parts[...].astype(f32), axis=0)).astype(bf16)
    out[...] = jnp.broadcast_to(new[None], out.shape)


def prepare_queries(keys, queries_t):
    put_queries(queries_t, keys, True)


def prepare_write(latents, lat, values, values_t):
    tiles, rows, _ = latents.shape
    for at in range(0, tiles, LN_ROWS // rows):
        new = latents[at : at + LN_ROWS // rows].astype(f32).reshape(LN_ROWS, WIDTH)
        to = slice(at * rows, at * rows + LN_ROWS)
        lat[to, :] = new.astype(bf16)
        values[to, :] = layer_norm(new).astype(bf16)
    put_values(values_t, values)


def write_first(
    latents, queries_t, tokens_hbm, peaks, totals, sums, tokens, lat, values, values_t, scores, weights, sem
):
    get = pltpu.make_async_copy(tokens_hbm, tokens, sem)
    get.start()
    prepare_write(latents, lat, values, values_t)
    attend(lat, queries_t, values_t, scores, weights, None, keep_in(peaks, totals, sums))
    get.wait()


def write_second(
    position, latents, mine, queries_t, tokens, peaks, totals, sums, out, owned,
    lat, values, values_t, scores, weights
):
    prepare_write(latents, lat, values, values_t)
    per = owned.shape[0]
    first = position[0] * per
    tiles = latents.shape[0]
    start = lax.rem(first, tiles)
    theirs = (lax.div(first, tiles) == position[1]).astype(jnp.int32) == 0

    @pl.when(theirs)
    def _():
        owned[...] = latents[pl.ds(start, per)]

    @pl.when(jnp.logical_not(theirs))
    def _():
        owned[...] = mine[pl.ds(start, per)]

    held = {}

    def then(head, peak, summed, total):
        held[head] = summed * (1.0 / total)
        if head % 2 == 1:
            both = jnp.concatenate([held[head - 1], held[head]], axis=0)
            pair = slice((head - 1) * HD, (head + 1) * HD)
            out[:, pair] = (tokens[:, pair].astype(f32) + both.T).astype(bf16)

    attend(
        lat, queries_t, values_t, scores, weights,
        lambda head: peaks[head : head + 1, :],
        joined(peaks, totals, sums, then),
    )


def call(kernel, outs, scratch=(), inputs=1, scalars=False, flops=0, far=(), far_out=False, limit=16 << 20):
    whole = pl.BlockSpec(memory_space=pltpu.VMEM)
    single = not isinstance(outs, (list, tuple))
    specs = [pl.BlockSpec(memory_space=pltpu.HBM) if i in far else whole for i in range(inputs)]
    out_specs = [whole] * (1 if single else len(outs))
    if far_out:
        out_specs[0] = pl.BlockSpec(memory_space=pltpu.HBM)
    if scalars:
        specs = [pl.BlockSpec(memory_space=pltpu.SMEM)] + specs
    return pl.pallas_call(
        kernel,
        out_shape=outs,
        in_specs=specs,
        out_specs=out_specs[0] if single else out_specs,
        scratch_shapes=list(scratch),
        compiler_params=pltpu.CompilerParams(vmem_limit_bytes=limit),
        name=kernel.__name__,
        cost_estimate=pl.CostEstimate(flops=flops, transcendentals=flops // 256, bytes_accessed=1 << 20),
    )


def on_device(tokens, latents, up_weight, down_weight):
    shape = jax.ShapeDtypeStruct
    n_space, n_z = lax.axis_size(SPACE), lax.axis_size(Z)
    count, width = tokens.shape
    half = latents.shape[0] // 2
    rows = half // n_space
    core, place = lax.axis_index(CORE), lax.axis_index(SPACE)
    position = jnp.stack([place, core]).astype(jnp.int32)
    heavy = 4 * half * count * width
    swap = [(0, 1), (1, 0)]

    def work(keys, queries):
        return [
            pltpu.VMEM((H, HD + ONES, keys), bf16),
            pltpu.VMEM((SLOTS, keys, queries), f32),
            pltpu.VMEM((SLOTS, keys, queries), bf16),
        ]

    def state(queries):
        return [shape((H, queries), f32), shape((H, queries), f32), shape((width, queries), f32)]

    block = lambda rows: pltpu.VMEM((rows, width), bf16)
    queries_t = call(
        prepare_read, shape((H, 2 * HD, half), bf16), [block(half), pltpu.SemaphoreType.DMA],
        inputs=1, scalars=True, flops=heavy // 8, far=(0,), limit=53248 << 10,
    )(position, latents)
    swapped, queries_t = lax.optimization_barrier((tokens, queries_t))
    other = lax.ppermute(swapped, CORE, swap)
    keys, *part = call(
        read_first, [shape((count, width), bf16), *state(half)],
        [block(count), *work(count, half), pltpu.SemaphoreType.DMA],
        inputs=2, flops=heavy, far_out=True,
    )(tokens, queries_t)
    tile = (n_space, rows, width + STATS)
    packed = call(
        read_second, shape(tile, bf16),
        [
            block(count), *work(count, half), pltpu.VMEM((STATS, half), f32), pltpu.VMEM(tile, bf16),
            pltpu.SemaphoreType.DMA((3,)),
        ],
        inputs=5, flops=heavy, far_out=True,
    )(other, queries_t, *part)
    packed, up_late, down_late, keys, late = lax.optimization_barrier(
        (packed, up_weight, down_weight, keys, latents)
    )
    packed = lax.all_to_all(packed, SPACE, 0, 0, tiled=True)
    up_other, down_other = lax.ppermute(up_late, CORE, swap), lax.ppermute(down_late, CORE, swap)
    queries_t = call(
        prepare_queries, shape((H, 4 * HD, count), bf16), flops=1 << 20, limit=53862 << 10
    )(keys)
    mine = lax.dynamic_slice_in_dim(late, core * half + place * rows, rows, 0)
    weights = [up_late, down_late, up_other, down_other]
    weights = call(
        hold, [shape(w.shape, bf16) for w in weights], [pltpu.SemaphoreType.DMA((4,))],
        inputs=4, flops=1 << 20, far=range(4), limit=52224 << 10,
    )(*weights)
    packed, queries_t, mine, *weights = lax.optimization_barrier((packed, queries_t, mine, *weights))
    tiles = call(combine_space, shape((n_z, rows, width + STATS), bf16))(packed)
    tiles = lax.all_to_all(tiles, Z, 0, 0, tiled=True)
    parts, middle = call(
        mlp, [shape((n_z, rows, width), bf16), shape((rows, width), f32)], inputs=6
    )(tiles, mine, *weights)
    parts = lax.all_to_all(parts, Z, 0, 0, tiled=True)
    new = call(finish, shape((n_space, rows, width), bf16), inputs=2)(parts, middle)
    mine = lax.all_to_all(new, SPACE, 0, 0, tiled=True)
    theirs = lax.ppermute(mine, CORE, swap)
    *part, held = call(
        write_first, [*state(count), shape((count, width), bf16)],
        [block(half), block(half), *work(half, count), pltpu.SemaphoreType.DMA],
        inputs=3, flops=heavy, far=(2,),
    )(mine, queries_t, tokens)
    new_tokens, new_latents = call(
        write_second,
        [shape((count, width), bf16), shape((2, rows, width), bf16)],
        [block(half), block(half), *work(half, count)],
        inputs=7, scalars=True, flops=heavy,
    )(position, theirs, mine, queries_t, held, *part)
    return (new_tokens, new_latents.reshape(2 * rows, width))


def solution(mesh):
    tm, space = mesh.shape["tm"], mesh.shape["space"]
    split = Mesh(
        mesh.devices.reshape(tm // 2, 2, space // 4, 4), ("tm_0", "tm_1", "space_0", "space_1")
    )
    in_specs = (P(TM_SPACE, None), P(), P(None, TM), P(TM, None))
    out_specs = (P(TM_SPACE, None), P(SPACE, None))
    return jax.shard_map(
        on_device, mesh=split, in_specs=in_specs, out_specs=out_specs, check_vma=False
    )
```
